256 devices in a mesh: dp: 128 (over z, y, x), sub: 2 (over core).
Axes of the slice: x: 4, y: 4, z: 8, core: 2. Of those that a mesh axis runs over, the one named last changes fastest.
Arguments:
- grads: bfloat16 [128, 2, 2048, 512], P('dp', None, 'sub'), may hold values from -84 to 84
- errors: bfloat16 [128, 2, 2048, 512], P('dp', None, 'sub'), may hold values from -3 to 3
- vec_grads: float32 [128, 2, 2048], P('dp', None, 'sub'), may hold values from -24 to 24
- gains: float32 [2, 2048], P(None, 'sub'), may hold values from 0.5 to 1.5
- q_start: float32 [2, 512, 32], replicated, may hold values from -0.25 to 0.25
- owner: int32 [256], replicated, may hold values from 0 to 127, as said below
- momentum: float32 [512, 16, 512], P('dp', None, 'sub'), may hold values from -3 to 3
- master: float32 [512, 16, 512], P('dp', None, 'sub'), may hold values from -5 to 5
Outputs:
- errors_out: bfloat16 [128, 2, 2048, 512], P('dp', None, 'sub')
- new_gains: float32 [2, 2048], P(None, 'sub')
- new_momentum: float32 [512, 16, 512], P('dp', None, 'sub')
- new_master: float32 [512, 16, 512], P('dp', None, 'sub')
- weights: bfloat16 [2, 2048, 512], P(None, None, 'sub')
The draws below stay inside these ranges and needn't reach their ends.
Inputs may be any that keep to these rules, and one draw needn't show every extreme that they name: `owner`: each dp index owns at most 4 blocks and some index owns exactly 4; momentum and master in empty slots are not used.
All inputs are finite; a program needn't handle non-finite values.
Results may differ from the reference program's by a relative error of at most 0.005.
Values may be sent and summed in bfloat16 or wider, within the bound.
A program may use at most 128 MiB of HBM per device.

```python
import jax
import jax.numpy as jnp
from jax import lax

D = 2048
KV = 512
MATS = 2
RANK = 32
ROUNDS = 2
VEC = 2
BR = 16
BLOCKS = 256
SLOTS = 4
N_DP = 128


def draw_grads(key, part):
    k_shared, k_rows, k_cols, k_noise = jax.random.split(jax.random.fold_in(key, 11), 4)
    shared = jax.random.truncated_normal(k_shared, -4.0, 4.0, (MATS, D, KV), jnp.float32)
    rows = jnp.exp(jax.random.uniform(k_rows, (MATS, D, 1), jnp.float32, jnp.log(0.3), jnp.log(3.0)))
    cols = jnp.exp(jax.random.uniform(k_cols, (MATS, 1, KV), jnp.float32, jnp.log(0.5), jnp.log(3.0)))
    cols = jnp.minimum(cols, 3.0)
    spread = 1.0 + 2.0 * jnp.arange(N_DP, dtype=jnp.float32) / max(N_DP - 1, 1)
    noise = jax.random.truncated_normal(k_noise, -4.0, 4.0, (N_DP, MATS, D, KV), jnp.float32)
    values = 0.5 * (shared * rows * cols)[None] + 4.0 * spread[:, None, None, None] * noise
    return jnp.clip(values, -84.0, 84.0).astype(jnp.bfloat16)


def draw_owner(key, part):
    k_first, k_order, k_shuffle = jax.random.split(jax.random.fold_in(key, 23), 3)
    chosen = jax.random.randint(k_first, (), 0, N_DP)
    tickets = jnp.arange(N_DP * SLOTS, dtype=jnp.int32)
    device = tickets // SLOTS
    scores = jax.random.permutation(k_order, N_DP * SLOTS).astype(jnp.int32)
    scores = jnp.where(device == chosen, -1 - tickets % SLOTS, scores)
    order = jnp.argsort(scores, stable=True)
    owners = device[order[:BLOCKS]]
    return jax.random.permutation(k_shuffle, owners).astype(jnp.int32)


def steps_of(own_key, extent, cuts, smallest, top_value):
    level = 1.0
    for axis_at, parts in cuts:
        draws = jax.random.uniform(jax.random.fold_in(jax.random.fold_in(own_key, 6), axis_at), (parts,), jnp.float32, smallest / len(cuts), top_value / len(cuts))
        level = level * jnp.repeat(jnp.exp(draws), extent[axis_at] // parts).reshape((-1,) + (1,) * (len(extent) - 1 - axis_at))
    return level


def scatter_about(stream_key, shape, deviation, most, shards=(), kind=jnp.bfloat16):
    level = steps_of(stream_key, shape, shards, -0.22, 0.18) if shards else 1.0
    entries = jax.random.normal(stream_key, shape, jnp.float32) * deviation * level
    return jnp.minimum(jnp.maximum(entries, -most), most).astype(kind)


def setup_inputs(seed: int = 0) -> dict:
    seeds = jax.random.split(jax.random.key(seed), 9)
    grads = draw_grads(jax.random.fold_in(seeds[8], 71), 0)
    errors = scatter_about(seeds[1], (N_DP, MATS, D, KV), 0.5, 3.0, ((0, 128), (2, 2)))
    vec_grads = scatter_about(seeds[2], (N_DP, VEC, D), 4.0, 24.0, ((0, 128), (2, 2)), jnp.float32)
    gains = jnp.clip(1.0 + 0.1 * jax.random.normal(seeds[3], (VEC, D), jnp.float32), 0.5, 1.5)
    q_start = scatter_about(seeds[4], (MATS, KV, RANK), KV ** -0.5, 0.25, (), jnp.float32)
    owner = draw_owner(jax.random.fold_in(seeds[8], 71), 0)
    momentum = scatter_about(seeds[6], (N_DP * SLOTS, BR, KV), 0.5, 3.0, ((0, 128), (2, 2)), jnp.float32)
    master = scatter_about(seeds[7], (N_DP * SLOTS, BR, KV), 1.0, 5.0, ((0, 128), (2, 2)), jnp.float32)
    return dict(grads=grads, errors=errors, vec_grads=vec_grads, gains=gains, q_start=q_start, owner=owner, momentum=momentum, master=master)


HIGH = lax.Precision.HIGHEST
momentum_decay = 0.9
step_rate = 0.5
vector_rate = 1.0

def replica_sum(grads, errors, fn, init):

    def step(total, pair):
        mixed = pair[0].astype(jnp.float32) + pair[1].astype(jnp.float32)
        return (total + fn(mixed), None)
    total, _ = lax.scan(step, init, (grads, errors))
    return total

def orthonormal(p):
    gram = jnp.einsum('mdr,mds->mrs', p, p, precision=HIGH)
    lower = jnp.linalg.cholesky(gram)
    return lax.linalg.triangular_solve(lower, p, left_side=False, lower=True, transpose_a=True)

def reference(grads, errors, vec_grads, gains, q_start, owner, momentum, master):
    new_gains = gains - vector_rate * (jnp.sum(vec_grads, axis=0) / N_DP)
    right = q_start
    for step_index in range(ROUNDS):
        left = replica_sum(grads, errors, lambda m: jnp.einsum('mdk,mkr->mdr', m, right, precision=HIGH), jnp.zeros((MATS, D, RANK), jnp.float32)) / N_DP
        basis = orthonormal(left)
        right = replica_sum(grads, errors, lambda m: jnp.einsum('mdk,mdr->mkr', m, basis, precision=HIGH), jnp.zeros((MATS, KV, RANK), jnp.float32)) / N_DP
    approx = jnp.einsum('mdr,mkr->mdk', basis, right, precision=HIGH)

    def error_row(pair):
        mixed = pair[0].astype(jnp.float32) + pair[1].astype(jnp.float32)
        return (mixed - approx).astype(jnp.bfloat16)
    errors_out = lax.map(error_row, (grads, errors))
    index = jnp.arange(BLOCKS, dtype=jnp.int32)
    same = owner[:, None] == owner[None, :]
    earlier = index[None, :] < index[:, None]
    rank = jnp.sum((same & earlier).astype(jnp.int32), axis=1).astype(jnp.int32)
    pos = (owner * SLOTS + rank).astype(jnp.int32)
    slot_block = jnp.zeros((N_DP * SLOTS,), jnp.int32).at[pos].set(index)
    valid = jnp.zeros((N_DP * SLOTS,), jnp.float32).at[pos].set(1.0)[:, None, None]
    approx_blocks = approx.reshape(BLOCKS, BR, KV)
    approx_slots = approx_blocks[slot_block] * valid
    new_momentum = (momentum_decay * momentum + approx_slots) * valid
    new_master = (master - step_rate * new_momentum) * valid
    weights = new_master[pos].reshape(MATS, D, KV).astype(jnp.bfloat16)
    return (errors_out, new_gains, new_momentum, new_master, weights)
```

```python
import functools

import jax
import jax.numpy as jnp
from jax import lax
from jax.experimental import pallas as pl
from jax.experimental.pallas import tpu as pltpu
from jax.sharding import PartitionSpec as P

MESH = pl.DeviceIdType.MESH
F32 = jnp.float32
BF16 = jnp.bfloat16
HIGH = lax.Precision.HIGHEST

ROUNDS = 2
MOMENTUM_DECAY = 0.9
STEP_RATE = 0.5
VECTOR_RATE = 1.0

LANES = 128
TILE = 8
BLOCK = 16
UNITS = 8

ORDERS = (((2, 1, 0), 0, 3), ((1, 0, 2), 3, 3), ((0, 2, 1), 6, 2))


def torus(dp):
    return {128: (8, 4, 4), 16: (4, 2, 2), 8: (2, 2, 2)}[dp]


def split3(value):
    high = value.astype(BF16)
    rest = value - high.astype(F32)
    middle = rest.astype(BF16)
    low = (rest - middle.astype(F32)).astype(BF16)
    return high, middle, low


def nt(a, b):
    return lax.dot_general(a, b, (((1,), (1,)), ((), ())), preferred_element_type=F32)


def nn(a, b):
    return lax.dot_general(a, b, (((1,), (0,)), ((), ())), preferred_element_type=F32)


def chains(n):
    found = []
    for longer in (True, False):
        for direction in (1, -1):
            half = 0 if (direction == 1) == longer else 1
            hops = n // 2 if longer else n // 2 - 1
            if hops:
                found.append((direction, half, hops))
    return found


def hop_table(n):
    table = {}
    for number, (_, _, hops) in enumerate(chains(n)):
        for hop in range(1, hops + 1):
            table[number, hop] = len(table)
    return table


def inverse_factor(gram0, gram1):
    rank = gram0.shape[0]
    rows = lax.broadcasted_iota(jnp.int32, (rank, LANES), 0)
    lanes = lax.broadcasted_iota(jnp.int32, (rank, LANES), 1)
    eye = (lax.broadcasted_iota(jnp.int32, (rank, rank), 0) == lax.broadcasted_iota(jnp.int32, (rank, rank), 1)).astype(F32)
    table = jnp.concatenate([gram0, eye, gram1, eye], axis=1)
    first = lanes < 2 * rank
    pivots = jnp.ones((rank, LANES), F32)
    for k in range(rank):
        column = jnp.where(first, table[:, k : k + 1], table[:, 2 * rank + k : 2 * rank + k + 1])
        pivot = column[k : k + 1, :]
        pivots = jnp.where(rows == k, pivot, pivots)
        if k < rank - 1:
            scaled = table[k : k + 1, :] / pivot
            table = table - jnp.where(rows > k, column * scaled, 0.0)
    table = table * lax.rsqrt(pivots)
    return table[:, rank : 2 * rank], table[:, 3 * rank : 4 * rank]


class Exchange:
    def __init__(self, sizes):
        self.sizes = sizes
        dp = lax.axis_index("dp")
        nz, ny, nx = sizes
        self.me = (dp // (ny * nx), (dp // nx) % ny, dp % nx)
        self.sub = lax.axis_index("sub")
        self.sent = []

    def peer(self, axis, step):
        n = self.sizes[axis]
        place = list(self.me)
        place[axis] = lax.rem(place[axis] + (step % n), n)
        return (place[0] * self.sizes[1] + place[1]) * self.sizes[2] + place[2]

    def place(self, axis, step):
        n = self.sizes[axis]
        return lax.rem(self.me[axis] + (step % n), n)

    def copy(self, source, target, send, receive, peer, sub=None):
        made = pltpu.make_async_remote_copy(
            src_ref=source,
            dst_ref=target,
            send_sem=send,
            recv_sem=receive,
            device_id=(peer, self.sub if sub is None else sub),
            device_id_type=MESH,
        )
        made.start()
        self.sent.append(made)
        return made

    def cut(self, axes, units, half=None):
        index = []
        for axis in range(3):
            if axis in axes:
                index.append(axes[axis])
            elif half is not None and axis == half[0]:
                n = self.sizes[axis]
                index.append(pl.ds(half[1] * (n // 2), n // 2))
            else:
                index.append(slice(None))
        index.append(pl.ds(units[0], units[1]))
        return tuple(index)


def ring_scatter(ex, buffer, landing, send, receive, order, units):
    axis = order[0]
    n = ex.sizes[axis]
    halved = 1 if axis == 0 else 0
    table = hop_table(n)
    links = chains(n)
    copies = {}

    def start(number, hop):
        direction, half, hops = links[number]
        target = ex.place(axis, direction * (hops - hop + 1))
        at = table[number, hop]
        copies[number, hop] = ex.copy(
            buffer.at[ex.cut({axis: target}, units, (halved, half))],
            landing.at[at],
            send.at[at],
            receive.at[at],
            ex.peer(axis, direction),
        )

    for number in range(len(links)):
        start(number, 1)
    for hop in range(1, n // 2 + 1):
        for number, (direction, half, hops) in enumerate(links):
            if hop > hops:
                continue
            yield
            copies[number, hop].wait_recv()
            target = ex.place(axis, direction * (hops - hop))
            index = ex.cut({axis: target}, units, (halved, half))
            buffer[index] = buffer[index] + landing[table[number, hop]]
            if hop < hops:
                start(number, hop + 1)


def direct_scatter(ex, buffer, landing, send, receive, order, stage, units):
    axis = order[stage]
    n = ex.sizes[axis]
    fixed = {a: ex.me[a] for a in order[:stage]}
    copies = []
    for step in range(1, n):
        index = ex.cut({**fixed, axis: ex.place(axis, step)}, units)
        copies.append(
            ex.copy(buffer.at[index], landing.at[step - 1], send.at[step - 1], receive.at[step - 1], ex.peer(axis, step))
        )
    yield
    own = ex.cut({**fixed, axis: ex.me[axis]}, units)
    total = buffer[own]
    for step in range(1, n):
        copies[step - 1].wait_recv()
        total = total + landing[step - 1]
    buffer[own] = total


def direct_gather(ex, buffer, send, receive, order, stage, units):
    axis = order[stage]
    n = ex.sizes[axis]
    index = ex.cut({a: ex.me[a] for a in order[: stage + 1]}, units)
    copies = []
    for step in range(1, n):
        copies.append(
            ex.copy(buffer.at[index], buffer.at[index], send.at[step - 1], receive.at[step - 1], ex.peer(axis, step))
        )
    yield
    for made in copies:
        made.wait_recv()


def ring_gather(ex, buffer, send, receive, order, units):
    axis = order[0]
    n = ex.sizes[axis]
    halved = 1 if axis == 0 else 0
    table = hop_table(n)
    links = chains(n)
    copies = {}

    def start(number, hop):
        direction, half, _ = links[number]
        index = ex.cut({axis: ex.place(axis, -direction * (hop - 1))}, units, (halved, half))
        at = table[number, hop]
        copies[number, hop] = ex.copy(
            buffer.at[index], buffer.at[index], send.at[at], receive.at[at], ex.peer(axis, direction)
        )

    for number in range(len(links)):
        start(number, 1)
    for hop in range(1, n // 2 + 1):
        for number, (_, _, hops) in enumerate(links):
            if hop > hops:
                continue
            yield
            copies[number, hop].wait_recv()
            if hop < hops:
                start(number, hop + 1)


def vector_sum(ex, buffer, landing, send, receive):
    at = 0
    for axis in (2, 1, 0):
        n = ex.sizes[axis]
        copies = []
        stage = 2 - axis
        for step in range(1, n):
            slot = at + step - 1
            copies.append(
                ex.copy(buffer.at[stage], landing.at[slot], send.at[slot], receive.at[slot], ex.peer(axis, step))
            )
        yield
        total = buffer[stage]
        for step in range(1, n):
            copies[step - 1].wait_recv()
            total = total + landing[at + step - 1]
        buffer[stage + 1] = total
        at += n - 1


def chain(*parts):
    for part in parts:
        yield from part()


def interleave(*parts):
    live = list(parts)
    while live:
        for part in list(live):
            try:
                next(part)
            except StopIteration:
                live.remove(part)


def drain(part, steps):
    for _ in range(steps):
        try:
            next(part)
        except StopIteration:
            return


def share_kernel(sizes, *refs):
    refs = list(refs)
    take = lambda count: [refs.pop(0) for _ in range(count)]
    grads, errors, vec_grads, q_start, momentum, master = take(6)
    basis_out, right_out, vec_out, slots_out = take(4)
    raw_g, raw_e, load_sem, work, mean = take(5)
    high, low = take(2)
    vec_buf, vec_land, vec_send, vec_recv = take(4)
    left_t = take(1)[0]
    mine, theirs, core_send, core_recv = take(4)
    basis_mine, basis_theirs = take(2)
    slots_mine = take(1)[0]
    lands, sends, recvs = [], [], []
    for _ in ORDERS:
        lands.append(take(3))
        sends.append(take(9))
        recvs.append(take(9))

    nz, ny, nx = sizes
    ex = Exchange(sizes)
    rank = q_start.shape[2]
    cols = q_start.shape[1]
    groups = cols // LANES
    plane = ny * nx * BLOCK
    per_mat = nz // 2
    dp_count = nz * ny * nx

    barrier = pltpu.get_barrier_semaphore()
    peers = [(ex.peer(axis, step), ex.sub) for axis in range(3) for step in range(1, sizes[axis])]
    peers.append((lax.axis_index("dp"), 1 - ex.sub))
    for peer in peers:
        pl.semaphore_signal(barrier, inc=1, device_id=peer, device_id_type=MESH)

    loads = []
    for z in range(nz):
        rows = pl.ds((z % per_mat) * plane, plane)
        pair = []
        for number, (source, target) in enumerate(((grads, raw_g), (errors, raw_e))):
            made = pltpu.make_async_copy(source.at[0, z // per_mat, rows], target.at[z], load_sem.at[z, number])
            made.start()
            pair.append(made)
        loads.append(pair)

    slots = master[...] - (STEP_RATE * MOMENTUM_DECAY) * momentum[...]
    slots = slots.astype(BF16)
    for slot in range(slots.shape[0]):
        for group in range(2):
            slots_mine[2 * slot + group] = slots[slot, :, group * LANES : (group + 1) * LANES]
    vec_buf[0] = vec_grads[0]
    own_slots = pltpu.make_async_copy(slots_mine, slots_out.at[ex.me[0], ex.me[1], ex.me[2]], load_sem.at[0, 2])
    own_slots.start()

    for z in range(nz):
        for made in loads[z]:
            made.wait()
        mixed = raw_g[z].astype(F32) + raw_e[z].astype(F32)
        for group in range(groups):
            tiles = mixed[:, group * LANES : (group + 1) * LANES].reshape(ny, nx, 2, TILE, LANES)
            work[z, :, :, 2 * group : 2 * group + 2] = tiles
    own_slots.wait()

    pl.semaphore_wait(barrier, len(peers))

    def scatter(number):
        order, first, count = ORDERS[number]
        units = (first, count)
        land, send, recv = lands[number], sends[number], recvs[number]
        yield from ring_scatter(ex, work, land[0], send[0], recv[0], order, units)
        yield from direct_scatter(ex, work, land[1], send[1], recv[1], order, 1, units)
        yield from direct_scatter(ex, work, land[2], send[2], recv[2], order, 2, units)
        own = ex.cut({a: ex.me[a] for a in range(3)}, units)
        mean[own] = work[own]
        yield from direct_gather(ex, mean, send[3], recv[3], order, 2, units)
        yield from direct_gather(ex, mean, send[4], recv[4], order, 1, units)
        yield from ring_gather(ex, mean, send[5], recv[5], order, units)

    def spread(number):
        order, first, count = ORDERS[number]
        units = (first, count)
        send, recv = sends[number], recvs[number]
        yield from direct_gather(ex, slots_out, send[6], recv[6], order, 2, units)
        yield from direct_gather(ex, slots_out, send[7], recv[7], order, 1, units)
        yield from ring_gather(ex, slots_out, send[8], recv[8], order, units)

    interleave(*[scatter(number) for number in range(3)], vector_sum(ex, vec_buf, vec_land, vec_send, vec_recv))
    vec_out[...] = vec_buf[3]
    spreads = [spread(number) for number in range(3)]

    def advance(steps=1):
        for _ in range(steps):
            for part in spreads:
                drain(part, 1)

    advance()
    scale = 1.0 / dp_count
    for z in range(nz):
        for group in range(groups):
            tiles = mean[z, :, :, 2 * group : 2 * group + 2].reshape(plane, LANES) * scale
            top = tiles.astype(BF16)
            high[z, :, group * LANES : (group + 1) * LANES] = top
            low[z, :, group * LANES : (group + 1) * LANES] = (tiles - top.astype(F32)).astype(BF16)
    advance()

    right_t = [q_start[m].T for m in range(2)]
    for step_index in range(ROUNDS):
        for m in range(2):
            q_terms = split3(right_t[m])
            q_all = jnp.concatenate(q_terms, axis=0)
            q_two = jnp.concatenate(q_terms[:2], axis=0)
            gram = jnp.zeros((3 * rank, 3 * rank), F32)
            product = jnp.zeros((3 * rank, cols), F32)
            product_low = jnp.zeros((2 * rank, cols), F32)
            for part in range(per_mat):
                z = m * per_mat + part
                top, rest = high[z], low[z]
                wide = nt(q_all, top)
                narrow = nt(q_two, rest)
                left = wide[:rank] + (wide[rank : 2 * rank] + wide[2 * rank :] + (narrow[:rank] + narrow[rank:]))
                left_t[m, :, part * plane : (part + 1) * plane] = left
                p_terms = split3(left)
                p_all = jnp.concatenate(p_terms, axis=0)
                p_two = jnp.concatenate(p_terms[:2], axis=0)
                gram = gram + nt(p_all, p_all)
                product = product + nn(p_all, top)
                product_low = product_low + nn(p_two, rest)
            total = product[:rank] + (
                product[rank : 2 * rank] + product[2 * rank :] + (product_low[:rank] + product_low[rank:])
            )
            mine[step_index, m, :, :cols] = total
            gram_rows = gram[:rank] + (gram[rank : 2 * rank] + gram[2 * rank :])
            square = gram_rows[:, :rank] + (gram_rows[:, rank : 2 * rank] + gram_rows[:, 2 * rank :])
            mine[step_index, m, :, cols:] = jnp.concatenate([square] * (LANES // rank), axis=1)
        made = ex.copy(
            mine.at[step_index],
            theirs.at[step_index],
            core_send.at[step_index],
            core_recv.at[step_index],
            lax.axis_index("dp"),
            1 - ex.sub,
        )
        advance()
        made.wait_recv()
        both = [mine[step_index, m] + theirs[step_index, m] for m in range(2)]
        inverses = inverse_factor(*[both[m][:, cols : cols + rank] for m in range(2)])
        right_t = [
            lax.dot_general(
                inverses[m], both[m][:, :cols], (((1,), (0,)), ((), ())), precision=HIGH, preferred_element_type=F32
            )
            for m in range(2)
        ]
        advance()
    for m in range(2):
        right_out[m] = right_t[m]
        basis_mine[m] = lax.dot_general(
            inverses[m], left_t[m], (((1,), (0,)), ((), ())), precision=HIGH, preferred_element_type=F32
        )
    made = ex.copy(
        basis_mine, basis_theirs, core_send.at[ROUNDS], core_recv.at[ROUNDS], lax.axis_index("dp"), 1 - ex.sub
    )
    for part in spreads:
        drain(part, 64)
    basis_out[ex.sub] = basis_mine[...]
    made.wait_recv()
    basis_out[1 - ex.sub] = basis_theirs[...]
    for made in ex.sent:
        made.wait_send()


def share(sizes, grads, errors, vec_grads, q_start, momentum, master):
    nz, ny, nx = sizes
    mats, rows, cols = grads.shape[1:]
    rank = q_start.shape[2]
    plane = ny * nx * BLOCK
    vmem = pl.BlockSpec(memory_space=pltpu.VMEM)
    anywhere = pl.BlockSpec(memory_space=pl.ANY)
    dma = pltpu.SemaphoreType.DMA
    wires = sum(n - 1 for n in sizes)
    scratch = [
        pltpu.VMEM((nz, plane, cols), BF16),
        pltpu.VMEM((nz, plane, cols), BF16),
        dma((nz, 3)),
        pltpu.VMEM((nz, ny, nx, UNITS, TILE, LANES), F32),
        pltpu.VMEM((nz, ny, nx, UNITS, TILE, LANES), F32),
        pltpu.VMEM((nz, plane, cols), BF16),
        pltpu.VMEM((nz, plane, cols), BF16),
        pltpu.VMEM((4,) + vec_grads.shape[1:], F32),
        pltpu.VMEM((wires,) + vec_grads.shape[1:], F32),
        dma((wires,)),
        dma((wires,)),
        pltpu.VMEM((mats, rank, rows), F32),
        pltpu.VMEM((ROUNDS, mats, rank, cols + LANES), F32),
        pltpu.VMEM((ROUNDS, mats, rank, cols + LANES), F32),
        dma((ROUNDS + 1,)),
        dma((ROUNDS + 1,)),
        pltpu.VMEM((mats, rank, rows), F32),
        pltpu.VMEM((mats, rank, rows), F32),
        pltpu.VMEM((UNITS, BLOCK, LANES), BF16),
    ]
    for order, _, count in ORDERS:
        first, second, third = order
        halved = 1 if first == 0 else 0
        shape = [sizes[a] // 2 if a == halved else sizes[a] for a in range(3) if a != first]
        hops = len(hop_table(sizes[first]))
        tail = (count, TILE, LANES)
        scratch.append(pltpu.VMEM((hops, *shape, *tail), F32))
        scratch.append(pltpu.VMEM((sizes[second] - 1, sizes[third], *tail), F32))
        scratch.append(pltpu.VMEM((sizes[third] - 1, *tail), F32))
        counts = [hops, sizes[second] - 1, sizes[third] - 1]
        counts = counts + counts[::-1] + counts[::-1]
        for _ in range(2):
            scratch.extend(dma((n,)) for n in counts)
    return pl.pallas_call(
        functools.partial(share_kernel, sizes),
        out_shape=(
            jax.ShapeDtypeStruct((2, mats, rank, rows), F32),
            jax.ShapeDtypeStruct((mats, rank, cols), F32),
            jax.ShapeDtypeStruct(vec_grads.shape[1:], F32),
            jax.ShapeDtypeStruct((nz, ny, nx, UNITS, BLOCK, LANES), BF16),
        ),
        in_specs=[anywhere, anywhere, vmem, vmem, vmem, vmem],
        out_specs=(vmem, vmem, vmem, anywhere),
        scratch_shapes=scratch,
        compiler_params=pltpu.CompilerParams(
            collective_id=0, has_side_effects=True, vmem_limit_bytes=56 * 1024 * 1024
        ),
        name="share",
    )(grads, errors, vec_grads, q_start, momentum, master)


def finish_kernel(steps, table, grads, errors, basis, right, gathered, momentum, master, vec, gains, *rest):
    errors_out, new_gains, new_momentum, new_master, weights, approx = rest
    step = pl.program_id(0)
    sub = table[0]
    blocks = approx.shape[0]
    slots = momentum.shape[0]
    per_mat = steps // 2
    mat = step // per_mat
    part = lax.rem(step, per_mat)
    rows = grads.shape[2]
    half_cols = weights.shape[2]

    def cat(values, first):
        top, middle, low = split3(values)
        return jnp.concatenate([top, top, middle, low] if first else [top, middle, top, top], axis=0)

    def product(left_t, right_t):
        return lax.dot_general(cat(left_t, True), cat(right_t, False), (((0,), (0,)), ((), ())), preferred_element_type=F32)

    local = basis[sub, mat, :, pl.ds(pl.multiple_of(part * rows, rows), rows)]
    mixed = grads[0, 0].astype(F32) + errors[0, 0].astype(F32)
    errors_out[0, 0] = (mixed - product(local, right[mat])).astype(BF16)

    half = part // (per_mat // 2)
    inner = lax.rem(part, per_mat // 2)
    wide = basis[half, mat, :, pl.ds(pl.multiple_of(inner * 2 * rows, 2 * rows), 2 * rows)]
    columns = right[mat, :, pl.ds(pl.multiple_of(sub * half_cols, half_cols), half_cols)]
    per_step = 2 * rows // BLOCK
    approx[pl.ds(step * per_step, per_step)] = product(wide, columns).reshape(per_step, BLOCK, half_cols)

    for number in range(per_step):
        block = step * per_step + number
        at = table[1 + block]
        for group in range(half_cols // LANES):
            lanes = slice(group * LANES, (group + 1) * LANES)
            value = gathered[at, group].astype(F32) - STEP_RATE * approx[block, :, lanes]
            weights[0, number * BLOCK : (number + 1) * BLOCK, lanes] = value.astype(BF16)

    @pl.when(step == steps - 1)
    def _():
        new_gains[...] = gains[...] - vec[...]
        for slot in range(slots):
            valid = table[1 + blocks + slots + slot] > 0
            moved = MOMENTUM_DECAY * momentum[slot] + approx[table[1 + blocks + slot]]
            moved = jnp.where(valid, moved, 0.0)
            new_momentum[slot] = moved
            new_master[slot] = jnp.where(valid, master[slot] - STEP_RATE * moved, 0.0)


def finish(steps, table, grads, errors, basis, right, gathered, momentum, master, vec, gains):
    mats, rows, cols = grads.shape[1:]
    blocks = 2 * mats * rows // BLOCK
    half_cols = momentum.shape[2]
    per_mat = steps // 2
    chunk = rows // per_mat
    moving = lambda i, t: (0, i // per_mat, i % per_mat, 0)
    whole = lambda shape: pl.BlockSpec(shape, lambda i, t: (0,) * len(shape))
    return pl.pallas_call(
        functools.partial(finish_kernel, steps),
        grid_spec=pltpu.PrefetchScalarGridSpec(
            num_scalar_prefetch=1,
            grid=(steps,),
            in_specs=[
                pl.BlockSpec((1, 1, chunk, cols), moving),
                pl.BlockSpec((1, 1, chunk, cols), moving),
                whole(basis.shape),
                whole(right.shape),
                whole(gathered.shape),
                whole(momentum.shape),
                whole(master.shape),
                whole(vec.shape),
                whole(gains.shape),
            ],
            out_specs=[
                pl.BlockSpec((1, 1, chunk, cols), moving),
                whole(gains.shape),
                whole(momentum.shape),
                whole(master.shape),
                pl.BlockSpec((1, 2 * chunk, half_cols), lambda i, t: (i // per_mat, i % per_mat, 0)),
            ],
            scratch_shapes=[pltpu.VMEM((blocks, BLOCK, half_cols), F32)],
        ),
        out_shape=(
            jax.ShapeDtypeStruct(grads.shape, BF16),
            jax.ShapeDtypeStruct(gains.shape, F32),
            jax.ShapeDtypeStruct(momentum.shape, F32),
            jax.ShapeDtypeStruct(master.shape, F32),
            jax.ShapeDtypeStruct((mats, 2 * rows, half_cols), BF16),
        ),
        compiler_params=pltpu.CompilerParams(vmem_limit_bytes=56 * 1024 * 1024),
        name="finish",
    )(table, grads, errors, basis, right, gathered, momentum, master, vec, gains)


def body(grads, errors, vec_grads, gains, q_start, owner, momentum, master):
    replicas = lax.axis_size("dp")
    sizes = torus(replicas)
    slots = momentum.shape[0]
    blocks = owner.shape[0]
    index = jnp.arange(blocks, dtype=jnp.int32)
    same = owner[:, None] == owner[None, :]
    earlier = index[None, :] < index[:, None]
    rank = jnp.sum((same & earlier).astype(jnp.int32), axis=1)
    pos = owner * slots + rank
    mine = (owner[None, :] == lax.axis_index("dp")) & (rank[None, :] == jnp.arange(slots, dtype=jnp.int32)[:, None])
    mine = mine.astype(jnp.int32)
    local_block = jnp.sum(mine * index[None, :], axis=1)
    valid = jnp.sum(mine, axis=1)
    table = jnp.concatenate([lax.axis_index("sub").astype(jnp.int32)[None], pos, local_block, valid])
    basis, right, vec, gathered = share(sizes, grads, errors, vec_grads, q_start, momentum, master)
    gathered = gathered.reshape(replicas * slots, 2, BLOCK, LANES)
    vec = vec * (VECTOR_RATE / replicas)
    errors_out, new_gains, new_momentum, new_master, weights = finish(
        sizes[0], table, grads, errors, basis, right, gathered, momentum, master, vec, gains
    )
    return (errors_out, new_gains, new_momentum, new_master, weights)


def solution(mesh):
    placed = (
        P("dp", None, "sub", None),
        P("dp", None, "sub", None),
        P("dp", None, "sub"),
        P(None, "sub"),
        P(),
        P(),
        P("dp", None, "sub"),
        P("dp", None, "sub"),
    )
    return jax.shard_map(
        body,
        mesh=mesh,
        in_specs=placed,
        out_specs=(
            P("dp", None, "sub", None),
            P(None, "sub"),
            P("dp", None, "sub"),
            P("dp", None, "sub"),
            P(None, None, "sub"),
        ),
        check_vma=False,
    )
```

```python
import functools

import jax
import jax.numpy as jnp
from jax import lax
from jax.experimental import pallas as pl
from jax.experimental.pallas import tpu as pltpu
from jax.sharding import PartitionSpec as P

MESH = pl.DeviceIdType.MESH
F32 = jnp.float32
BF16 = jnp.bfloat16
HIGH = lax.Precision.HIGHEST

ROUNDS = 2
MOMENTUM_DECAY = 0.9
STEP_RATE = 0.5
VECTOR_RATE = 1.0

LANES = 128
BLOCK = 16
UNITS = 8
PARTS = 4

ORDERS = (((2, 1, 0), (0, 2), (0, 3)), ((1, 0, 2), (2, 1), (3, 3)), ((0, 2, 1), (3, 1), (6, 2)))


def torus(dp):
    return {128: (8, 4, 4), 16: (4, 2, 2), 8: (2, 2, 2)}[dp]


def split3(value):
    high = value.astype(BF16)
    rest = value - high.astype(F32)
    middle = rest.astype(BF16)
    low = (rest - middle.astype(F32)).astype(BF16)
    return high, middle, low


def nt(a, b):
    return lax.dot_general(a, b, (((1,), (1,)), ((), ())), preferred_element_type=F32)


def nn(a, b):
    return lax.dot_general(a, b, (((1,), (0,)), ((), ())), preferred_element_type=F32)


def chains(n):
    found = []
    for longer in (True, False):
        for direction in (1, -1):
            half = 0 if (direction == 1) == longer else 1
            hops = n // 2 if longer else n // 2 - 1
            if hops:
                found.append((direction, half, hops))
    return found


def hop_table(n):
    table = {}
    for number, (_, _, hops) in enumerate(chains(n)):
        for hop in range(1, hops + 1):
            table[number, hop] = len(table)
    return table


def inverse_factor(gram0, gram1):
    rank = gram0.shape[0]
    rows = lax.broadcasted_iota(jnp.int32, (rank, LANES), 0)
    lanes = lax.broadcasted_iota(jnp.int32, (rank, LANES), 1)
    eye = (lax.broadcasted_iota(jnp.int32, (rank, rank), 0) == lax.broadcasted_iota(jnp.int32, (rank, rank), 1)).astype(F32)
    table = jnp.concatenate([gram0, eye, gram1, eye], axis=1)
    first = lanes < 2 * rank
    pivots = jnp.ones((rank, LANES), F32)
    for k in range(rank):
        column = jnp.where(first, table[:, k : k + 1], table[:, 2 * rank + k : 2 * rank + k + 1])
        pivot = column[k : k + 1, :]
        pivots = jnp.where(rows == k, pivot, pivots)
        if k < rank - 1:
            scaled = table[k : k + 1, :] / pivot
            table = table - jnp.where(rows > k, column * scaled, 0.0)
    table = table * lax.rsqrt(pivots)
    return table[:, rank : 2 * rank], table[:, 3 * rank : 4 * rank]


class Exchange:
    def __init__(self, sizes):
        self.sizes = sizes
        dp = lax.axis_index("dp")
        nz, ny, nx = sizes
        self.me = (dp // (ny * nx), (dp // nx) % ny, dp % nx)
        self.sub = lax.axis_index("sub")
        self.sent = []

    def peer(self, axis, step):
        n = self.sizes[axis]
        place = list(self.me)
        place[axis] = lax.rem(place[axis] + (step % n), n)
        return (place[0] * self.sizes[1] + place[1]) * self.sizes[2] + place[2]

    def place(self, axis, step):
        n = self.sizes[axis]
        return lax.rem(self.me[axis] + (step % n), n)

    def copy(self, source, target, send, receive, peer, sub=None):
        made = pltpu.make_async_remote_copy(
            src_ref=source,
            dst_ref=target,
            send_sem=send,
            recv_sem=receive,
            device_id=(peer, self.sub if sub is None else sub),
            device_id_type=MESH,
        )
        made.start()
        self.sent.append(made)
        return made

    def cut(self, axes, units, half=None):
        index = []
        for axis in range(3):
            if axis in axes:
                index.append(axes[axis])
            elif half is not None and axis == half[0]:
                n = self.sizes[axis]
                index.append(pl.ds(half[1] * (n // 2), n // 2))
            else:
                index.append(slice(None))
        index.append(pl.ds(units[0], units[1]))
        return tuple(index)


def ring_scatter(ex, buffer, wire, landing, send, receive, order, units):
    axis = order[0]
    n = ex.sizes[axis]
    halved = 1 if axis == 0 else 0
    table = hop_table(n)
    links = chains(n)
    copies = {}

    def start(number, hop):
        direction, half, hops = links[number]
        target = ex.place(axis, direction * (hops - hop + 1))
        at = table[number, hop]
        copies[number, hop] = ex.copy(
            wire.at[ex.cut({axis: target}, units, (halved, half))],
            landing.at[at],
            send.at[at],
            receive.at[at],
            ex.peer(axis, direction),
        )

    for number in range(len(links)):
        start(number, 1)
    for hop in range(1, n // 2 + 1):
        for number, (direction, half, hops) in enumerate(links):
            if hop > hops:
                continue
            yield
            copies[number, hop].wait_recv()
            target = ex.place(axis, direction * (hops - hop))
            index = ex.cut({axis: target}, units, (halved, half))
            total = buffer[index] + landing[table[number, hop]].astype(F32)
            if hop < hops:
                wire[index] = total.astype(BF16)
                start(number, hop + 1)
            else:
                buffer[index] = total


def direct_scatter(ex, buffer, wire, landing, send, receive, order, stage, units):
    axis = order[stage]
    n = ex.sizes[axis]
    fixed = {a: ex.me[a] for a in order[:stage]}
    copies = []
    for step in range(1, n):
        index = ex.cut({**fixed, axis: ex.place(axis, step)}, units)
        wire[index] = buffer[index].astype(BF16)
        copies.append(
            ex.copy(wire.at[index], landing.at[step - 1], send.at[step - 1], receive.at[step - 1], ex.peer(axis, step))
        )
    yield
    own = ex.cut({**fixed, axis: ex.me[axis]}, units)
    total = buffer[own]
    for step in range(1, n):
        copies[step - 1].wait_recv()
        total = total + landing[step - 1].astype(F32)
    buffer[own] = total


def direct_gather(ex, buffer, send, receive, order, stage, units):
    axis = order[stage]
    n = ex.sizes[axis]
    index = ex.cut({a: ex.me[a] for a in order[: stage + 1]}, units)
    copies = []
    for step in range(1, n):
        copies.append(
            ex.copy(buffer.at[index], buffer.at[index], send.at[step - 1], receive.at[step - 1], ex.peer(axis, step))
        )
    yield
    for made in copies:
        made.wait_recv()


def ring_gather(ex, buffer, send, receive, order, units):
    axis = order[0]
    n = ex.sizes[axis]
    halved = 1 if axis == 0 else 0
    table = hop_table(n)
    links = chains(n)
    copies = {}

    def start(number, hop):
        direction, half, _ = links[number]
        index = ex.cut({axis: ex.place(axis, -direction * (hop - 1))}, units, (halved, half))
        at = table[number, hop]
        copies[number, hop] = ex.copy(
            buffer.at[index], buffer.at[index], send.at[at], receive.at[at], ex.peer(axis, direction)
        )

    for number in range(len(links)):
        start(number, 1)
    for hop in range(1, n // 2 + 1):
        for number, (_, _, hops) in enumerate(links):
            if hop > hops:
                continue
            yield
            copies[number, hop].wait_recv()
            if hop < hops:
                start(number, hop + 1)


def vector_sum(ex, buffer, landing, send, receive):
    at = 0
    for axis in (2, 1, 0):
        n = ex.sizes[axis]
        copies = []
        stage = 2 - axis
        for step in range(1, n):
            slot = at + step - 1
            copies.append(
                ex.copy(buffer.at[stage], landing.at[slot], send.at[slot], receive.at[slot], ex.peer(axis, step))
            )
        yield
        total = buffer[stage]
        for step in range(1, n):
            copies[step - 1].wait_recv()
            total = total + landing[at + step - 1]
        buffer[stage + 1] = total
        at += n - 1


def chain(*parts):
    for part in parts:
        yield from part()


def interleave(*parts):
    live = list(parts)
    while live:
        for part in list(live):
            try:
                next(part)
            except StopIteration:
                live.remove(part)


def drain(part, steps):
    for _ in range(steps):
        try:
            next(part)
        except StopIteration:
            return


def share_kernel(sizes, *refs):
    refs = list(refs)
    take = lambda count: [refs.pop(0) for _ in range(count)]
    grads, errors, vec_grads, q_start, momentum, master = take(6)
    basis_out, right_out, vec_out, slots_out = take(4)
    raw_g, raw_e, load_sem, work, wire, mean = take(6)
    high = take(1)[0]
    vec_buf, vec_land, vec_send, vec_recv = take(4)
    left_t = take(1)[0]
    mine, theirs, core_send, core_recv = take(4)
    basis_mine, basis_theirs = take(2)
    slots_mine = take(1)[0]
    lands, sends, recvs = [], [], []
    for _ in ORDERS:
        lands.append(take(3))
        sends.append(take(9))
        recvs.append(take(9))

    nz, ny, nx = sizes
    ex = Exchange(sizes)
    rank = q_start.shape[1]
    cols = q_start.shape[2]
    groups = cols // LANES
    plane = ny * nx * BLOCK
    per_mat = nz // 2
    dp_count = nz * ny * nx

    barrier = pltpu.get_barrier_semaphore()
    peers = [(ex.peer(axis, step), ex.sub) for axis in range(3) for step in range(1, sizes[axis])]
    peers.append((lax.axis_index("dp"), 1 - ex.sub))
    for peer in peers:
        pl.semaphore_signal(barrier, inc=1, device_id=peer, device_id_type=MESH)

    loads = []
    for z in range(nz):
        rows = pl.ds((z % per_mat) * plane, plane)
        pair = []
        for number, (source, target) in enumerate(((grads, raw_g), (errors, raw_e))):
            made = pltpu.make_async_copy(source.at[0, z // per_mat, rows], target.at[z], load_sem.at[z, number])
            made.start()
            pair.append(made)
        loads.append(pair)

    slots = master[...] - (STEP_RATE * MOMENTUM_DECAY) * momentum[...]
    slots = slots.astype(BF16)
    for slot in range(slots.shape[0]):
        for group in range(2):
            slots_mine[2 * slot + group] = slots[slot, :, group * LANES : (group + 1) * LANES]
    vec_buf[0] = vec_grads[0]
    own_slots = pltpu.make_async_copy(slots_mine, slots_out.at[ex.me[0], ex.me[1], ex.me[2]], load_sem.at[0, 2])
    own_slots.start()

    for z in range(nz):
        for made in loads[z]:
            made.wait()
        mixed = raw_g[z].astype(F32) + raw_e[z].astype(F32)
        for group in range(groups):
            tiles = mixed[:, group * LANES : (group + 1) * LANES].reshape(ny, nx, BLOCK, LANES)
            work[z, :, :, group] = tiles
            wire[z, :, :, group] = tiles.astype(BF16)
    own_slots.wait()

    pl.semaphore_wait(barrier, len(peers))

    scale = 1.0 / dp_count
    gathered = [False] * len(ORDERS)

    def scatter(number):
        order, units, _ = ORDERS[number]
        land, send, recv = lands[number], sends[number], recvs[number]
        yield from ring_scatter(ex, work, wire, land[0], send[0], recv[0], order, units)
        yield from direct_scatter(ex, work, wire, land[1], send[1], recv[1], order, 1, units)
        yield from direct_scatter(ex, work, wire, land[2], send[2], recv[2], order, 2, units)
        own = ex.cut({a: ex.me[a] for a in range(3)}, units)
        mean[own] = (work[own] * scale).astype(BF16)
        yield from direct_gather(ex, mean, send[3], recv[3], order, 2, units)
        yield from direct_gather(ex, mean, send[4], recv[4], order, 1, units)
        yield from ring_gather(ex, mean, send[5], recv[5], order, units)
        assert gathered[number]
        next(spreads[number])

    def early(number):
        order, _, units = ORDERS[number]
        send, recv = sends[number], recvs[number]
        yield from direct_gather(ex, slots_out, send[6], recv[6], order, 2, units)
        yield from direct_gather(ex, slots_out, send[7], recv[7], order, 1, units)
        gathered[number] = True

    def spread(number):
        order, _, units = ORDERS[number]
        yield from ring_gather(ex, slots_out, sends[number][8], recvs[number][8], order, units)

    spreads = [spread(number) for number in range(3)]
    interleave(
        *[scatter(number) for number in range(3)],
        vector_sum(ex, vec_buf, vec_land, vec_send, vec_recv),
        *[early(number) for number in range(3)],
    )
    vec_out[...] = vec_buf[3] * (VECTOR_RATE / dp_count)

    def advance():
        for part in spreads:
            drain(part, 4)

    for z in range(nz):
        for group in range(groups):
            high[z, :, group * LANES : (group + 1) * LANES] = mean[z, :, :, group].reshape(plane, LANES)

    right_t = [q_start[m] for m in range(2)]
    for step_index in range(ROUNDS):
        for m in range(2):
            q_terms = split3(right_t[m])
            q_all = jnp.concatenate(q_terms, axis=0)
            gram = jnp.zeros((3 * rank, 3 * rank), F32)
            product = jnp.zeros((3 * rank, cols), F32)
            for part in range(per_mat):
                z = m * per_mat + part
                top = high[z]
                wide = nt(q_all, top)
                left = wide[:rank] + (wide[rank : 2 * rank] + wide[2 * rank :])
                left_t[m, :, part * plane : (part + 1) * plane] = left
                p_terms = split3(left)
                p_all = jnp.concatenate(p_terms, axis=0)
                gram = gram + nt(p_all, p_all)
                product = product + nn(p_all, top)
            total = product[:rank] + (product[rank : 2 * rank] + product[2 * rank :])
            mine[step_index, m, :, :cols] = total
            gram_rows = gram[:rank] + (gram[rank : 2 * rank] + gram[2 * rank :])
            square = gram_rows[:, :rank] + (gram_rows[:, rank : 2 * rank] + gram_rows[:, 2 * rank :])
            mine[step_index, m, :, cols:] = jnp.concatenate([square] * (LANES // rank), axis=1)
        made = ex.copy(
            mine.at[step_index],
            theirs.at[step_index],
            core_send.at[step_index],
            core_recv.at[step_index],
            lax.axis_index("dp"),
            1 - ex.sub,
        )
        advance()
        made.wait_recv()
        both = [mine[step_index, m] + theirs[step_index, m] for m in range(2)]
        inverses = inverse_factor(*[both[m][:, cols : cols + rank] for m in range(2)])
        right_t = [
            lax.dot_general(
                inverses[m], both[m][:, :cols], (((1,), (0,)), ((), ())), precision=HIGH, preferred_element_type=F32
            )
            for m in range(2)
        ]
        advance()
    for m in range(2):
        right_out[m] = right_t[m]
        basis_mine[m] = lax.dot_general(
            inverses[m], left_t[m], (((1,), (0,)), ((), ())), precision=HIGH, preferred_element_type=F32
        )
    made = ex.copy(
        basis_mine, basis_theirs, core_send.at[ROUNDS], core_recv.at[ROUNDS], lax.axis_index("dp"), 1 - ex.sub
    )
    for part in spreads:
        drain(part, 64)
    basis_out[ex.sub] = basis_mine[...]
    made.wait_recv()
    basis_out[1 - ex.sub] = basis_theirs[...]
    for made in ex.sent:
        made.wait_send()


def share(sizes, grads, errors, vec_grads, q_start, momentum, master):
    nz, ny, nx = sizes
    mats, rows, cols = grads.shape[1:]
    rank = q_start.shape[1]
    plane = ny * nx * BLOCK
    vmem = pl.BlockSpec(memory_space=pltpu.VMEM)
    anywhere = pl.BlockSpec(memory_space=pl.ANY)
    dma = pltpu.SemaphoreType.DMA
    wires = sum(n - 1 for n in sizes)
    scratch = [
        pltpu.VMEM((nz, plane, cols), BF16),
        pltpu.VMEM((nz, plane, cols), BF16),
        dma((nz, 3)),
        pltpu.VMEM((nz, ny, nx, PARTS, BLOCK, LANES), F32),
        pltpu.VMEM((nz, ny, nx, PARTS, BLOCK, LANES), BF16),
        pltpu.VMEM((nz, ny, nx, PARTS, BLOCK, LANES), BF16),
        pltpu.VMEM((nz, plane, cols), BF16),
        pltpu.VMEM((4,) + vec_grads.shape[1:], F32),
        pltpu.VMEM((wires,) + vec_grads.shape[1:], F32),
        dma((wires,)),
        dma((wires,)),
        pltpu.VMEM((mats, rank, rows), F32),
        pltpu.VMEM((ROUNDS, mats, rank, cols + LANES), F32),
        pltpu.VMEM((ROUNDS, mats, rank, cols + LANES), F32),
        dma((ROUNDS + 1,)),
        dma((ROUNDS + 1,)),
        pltpu.VMEM((mats, rank, rows), F32),
        pltpu.VMEM((mats, rank, rows), F32),
        pltpu.VMEM((UNITS, BLOCK, LANES), BF16),
    ]
    for order, (_, count), _ in ORDERS:
        first, second, third = order
        halved = 1 if first == 0 else 0
        shape = [sizes[a] // 2 if a == halved else sizes[a] for a in range(3) if a != first]
        hops = len(hop_table(sizes[first]))
        tail = (count, BLOCK, LANES)
        scratch.append(pltpu.VMEM((hops, *shape, *tail), BF16))
        scratch.append(pltpu.VMEM((sizes[second] - 1, sizes[third], *tail), BF16))
        scratch.append(pltpu.VMEM((sizes[third] - 1, *tail), BF16))
        counts = [hops, sizes[second] - 1, sizes[third] - 1]
        counts = counts + counts[::-1] + counts[::-1]
        for _ in range(2):
            scratch.extend(dma((n,)) for n in counts)
    return pl.pallas_call(
        functools.partial(share_kernel, sizes),
        out_shape=(
            jax.ShapeDtypeStruct((2, mats, rank, rows), F32),
            jax.ShapeDtypeStruct((mats, rank, cols), F32),
            jax.ShapeDtypeStruct(vec_grads.shape[1:], F32),
            jax.ShapeDtypeStruct((nz, ny, nx, UNITS, BLOCK, LANES), BF16),
        ),
        in_specs=[anywhere, anywhere, vmem, vmem, vmem, vmem],
        out_specs=(vmem, vmem, vmem, anywhere),
        scratch_shapes=scratch,
        compiler_params=pltpu.CompilerParams(
            collective_id=0, has_side_effects=True, vmem_limit_bytes=56 * 1024 * 1024
        ),
        name="share",
    )(grads, errors, vec_grads, q_start, momentum, master)


def finish_kernel(steps, table, grads, errors, basis, right, gathered, momentum, master, vec, gains, *rest):
    errors_out, new_gains, new_momentum, new_master, weights, approx = rest
    step = pl.program_id(0)
    sub = table[0]
    blocks = approx.shape[0]
    slots = momentum.shape[0]
    per_mat = steps // 2
    mat = step // per_mat
    part = lax.rem(step, per_mat)
    rows = grads.shape[2]
    half_cols = weights.shape[2]

    def cat(values, first):
        top, middle, low = split3(values)
        return jnp.concatenate([top, top, middle, low] if first else [top, middle, top, top], axis=0)

    def product(left_t, right_t):
        return lax.dot_general(cat(left_t, True), cat(right_t, False), (((0,), (0,)), ((), ())), preferred_element_type=F32)

    local = basis[sub, mat, :, pl.ds(pl.multiple_of(part * rows, rows), rows)]
    mixed = grads[0, 0].astype(F32) + errors[0, 0].astype(F32)
    errors_out[0, 0] = (mixed - product(local, right[mat])).astype(BF16)

    half = part // (per_mat // 2)
    inner = lax.rem(part, per_mat // 2)
    wide = basis[half, mat, :, pl.ds(pl.multiple_of(inner * 2 * rows, 2 * rows), 2 * rows)]
    columns = right[mat, :, pl.ds(pl.multiple_of(sub * half_cols, half_cols), half_cols)]
    per_step = 2 * rows // BLOCK
    approx[pl.ds(step * per_step, per_step)] = product(wide, columns).reshape(per_step, BLOCK, half_cols)

    for number in range(per_step):
        block = step * per_step + number
        at = table[1 + block]
        for group in range(half_cols // LANES):
            lanes = slice(group * LANES, (group + 1) * LANES)
            value = gathered[at, group].astype(F32) - STEP_RATE * approx[block, :, lanes]
            weights[0, number * BLOCK : (number + 1) * BLOCK, lanes] = value.astype(BF16)

    @pl.when(step == steps - 1)
    def _():
        new_gains[...] = gains[...] - vec[...]
        for slot in range(slots):
            valid = table[1 + blocks + slots + slot] > 0
            moved = MOMENTUM_DECAY * momentum[slot] + approx[table[1 + blocks + slot]]
            moved = jnp.where(valid, moved, 0.0)
            new_momentum[slot] = moved
            new_master[slot] = jnp.where(valid, master[slot] - STEP_RATE * moved, 0.0)


def finish(steps, table, grads, errors, basis, right, gathered, momentum, master, vec, gains):
    mats, rows, cols = grads.shape[1:]
    blocks = 2 * mats * rows // BLOCK
    half_cols = momentum.shape[2]
    per_mat = steps // 2
    chunk = rows // per_mat
    moving = lambda i, t: (0, i // per_mat, i % per_mat, 0)
    whole = lambda shape: pl.BlockSpec(shape, lambda i, t: (0,) * len(shape))
    return pl.pallas_call(
        functools.partial(finish_kernel, steps),
        grid_spec=pltpu.PrefetchScalarGridSpec(
            num_scalar_prefetch=1,
            grid=(steps,),
            in_specs=[
                pl.BlockSpec((1, 1, chunk, cols), moving),
                pl.BlockSpec((1, 1, chunk, cols), moving),
                whole(basis.shape),
                whole(right.shape),
                whole(gathered.shape),
                whole(momentum.shape),
                whole(master.shape),
                whole(vec.shape),
                whole(gains.shape),
            ],
            out_specs=[
                pl.BlockSpec((1, 1, chunk, cols), moving),
                whole(gains.shape),
                whole(momentum.shape),
                whole(master.shape),
                pl.BlockSpec((1, 2 * chunk, half_cols), lambda i, t: (i // per_mat, i % per_mat, 0)),
            ],
            scratch_shapes=[pltpu.VMEM((blocks, BLOCK, half_cols), F32)],
        ),
        out_shape=(
            jax.ShapeDtypeStruct(grads.shape, BF16),
            jax.ShapeDtypeStruct(gains.shape, F32),
            jax.ShapeDtypeStruct(momentum.shape, F32),
            jax.ShapeDtypeStruct(master.shape, F32),
            jax.ShapeDtypeStruct((mats, 2 * rows, half_cols), BF16),
        ),
        compiler_params=pltpu.CompilerParams(vmem_limit_bytes=56 * 1024 * 1024),
        name="finish",
    )(table, grads, errors, basis, right, gathered, momentum, master, vec, gains)


def body(grads, errors, vec_grads, gains, q_start, owner, momentum, master):
    replicas = lax.axis_size("dp")
    sizes = torus(replicas)
    slots = momentum.shape[0]
    blocks = owner.shape[0]
    index = jnp.arange(blocks, dtype=jnp.int32)
    same = owner[:, None] == owner[None, :]
    earlier = index[None, :] < index[:, None]
    rank = jnp.sum((same & earlier).astype(jnp.int32), axis=1)
    pos = owner * slots + rank
    mine = (owner[None, :] == lax.axis_index("dp")) & (rank[None, :] == jnp.arange(slots, dtype=jnp.int32)[:, None])
    mine = mine.astype(jnp.int32)
    local_block = jnp.sum(mine * index[None, :], axis=1)
    valid = jnp.sum(mine, axis=1)
    table = jnp.concatenate([lax.axis_index("sub").astype(jnp.int32)[None], pos, local_block, valid])
    basis, right, vec, gathered = share(
        sizes, grads, errors, vec_grads, jnp.swapaxes(q_start, 1, 2), momentum, master
    )
    gathered = gathered.reshape(replicas * slots, 2, BLOCK, LANES)
    errors_out, new_gains, new_momentum, new_master, weights = finish(
        sizes[0], table, grads, errors, basis, right, gathered, momentum, master, vec, gains
    )
    return (errors_out, new_gains, new_momentum, new_master, weights)


def solution(mesh):
    placed = (
        P("dp", None, "sub", None),
        P("dp", None, "sub", None),
        P("dp", None, "sub"),
        P(None, "sub"),
        P(),
        P(),
        P("dp", None, "sub"),
        P("dp", None, "sub"),
    )
    return jax.shard_map(
        body,
        mesh=mesh,
        in_specs=placed,
        out_specs=(
            P("dp", None, "sub", None),
            P(None, "sub"),
            P("dp", None, "sub"),
            P("dp", None, "sub"),
            P(None, None, "sub"),
        ),
        check_vma=False,
    )
```

```python
import functools

import jax
import jax.numpy as jnp
from jax import lax
from jax.experimental import pallas as pl
from jax.experimental.pallas import tpu as pltpu
from jax.sharding import PartitionSpec as P

MESH = pl.DeviceIdType.MESH
F32 = jnp.float32
BF16 = jnp.bfloat16
HIGH = lax.Precision.HIGHEST

ROUNDS = 2
MOMENTUM_DECAY = 0.9
STEP_RATE = 0.5
VECTOR_RATE = 1.0

LANES = 128
BLOCK = 16
UNITS = 8
STRIDE = 4
PARTS = 4

SLOT_ORDERS = ((2, 1, 0), (1, 2, 0), (0, 2, 1))

ORDERS = (((2, 1, 0), (0, 2), (0, 3)), ((1, 0, 2), (2, 1), (3, 3)), ((0, 2, 1), (3, 1), (6, 2)))


def torus(dp):
    return {128: (8, 4, 4), 16: (4, 2, 2), 8: (2, 2, 2)}[dp]


def split3(value):
    high = value.astype(BF16)
    rest = value - high.astype(F32)
    middle = rest.astype(BF16)
    low = (rest - middle.astype(F32)).astype(BF16)
    return high, middle, low


def nt(a, b):
    return lax.dot_general(a, b, (((1,), (1,)), ((), ())), preferred_element_type=F32)


def nn(a, b):
    return lax.dot_general(a, b, (((1,), (0,)), ((), ())), preferred_element_type=F32)


def chains(n):
    found = []
    for longer in (True, False):
        for direction in (1, -1):
            half = 0 if (direction == 1) == longer else 1
            hops = n // 2 if longer else n // 2 - 1
            if hops:
                found.append((direction, half, hops))
    return found


def hop_table(n):
    table = {}
    for number, (_, _, hops) in enumerate(chains(n)):
        for hop in range(1, hops + 1):
            table[number, hop] = len(table)
    return table


def inverse_factor(gram0, gram1):
    rank = gram0.shape[0]
    rows = lax.broadcasted_iota(jnp.int32, (rank, LANES), 0)
    lanes = lax.broadcasted_iota(jnp.int32, (rank, LANES), 1)
    eye = (lax.broadcasted_iota(jnp.int32, (rank, rank), 0) == lax.broadcasted_iota(jnp.int32, (rank, rank), 1)).astype(F32)
    table = jnp.concatenate([gram0, eye, gram1, eye], axis=1)
    first = lanes < 2 * rank
    pivots = jnp.ones((rank, LANES), F32)
    for k in range(0, rank, STRIDE):
        columns, lines = [], []
        for j in range(k, k + STRIDE):
            columns.append(jnp.where(first, table[:, j : j + 1], table[:, 2 * rank + j : 2 * rank + j + 1]))
            lines.append(table[j : j + 1, :])
        change = jnp.zeros((rank, LANES), F32)
        for j in range(STRIDE):
            pivot = columns[j][k + j : k + j + 1, :]
            pivots = jnp.where(rows == k + j, pivot, pivots)
            inverse = 1.0 / pivot
            scaled = lines[j] * inverse
            for i in range(j + 1, STRIDE):
                factor = columns[j][k + i : k + i + 1, :]
                lines[i] = lines[i] - factor * scaled
                columns[i] = columns[i] - columns[j] * (factor * inverse)
            change = change + jnp.where(rows > k + j, columns[j] * scaled, 0.0)
        table = table - change
    table = table * lax.rsqrt(pivots)
    return table[:, rank : 2 * rank], table[:, 3 * rank : 4 * rank]


def place_blocks(owner, dp, sub, slots):
    blocks = owner.shape[1]
    wide = jnp.broadcast_to(owner.astype(F32), (blocks, blocks))
    before = lax.broadcasted_iota(jnp.int32, wide.shape, 0)
    block = lax.broadcasted_iota(jnp.int32, wide.shape, 1)
    rank = jnp.sum(jnp.where((wide == wide.T) & (before < block), 1.0, 0.0), axis=0, keepdims=True)
    rank = rank.astype(jnp.int32)
    lines = [owner * slots + rank]
    for slot in range(slots):
        held = jnp.where((owner == dp) & (rank == slot), block[:1] + 1, 0).astype(F32)
        held = jnp.sum(held, axis=1, keepdims=True).astype(jnp.int32) - 1
        lines.append(jnp.broadcast_to(held, (1, blocks)))
    lines.append(jnp.broadcast_to(sub, (1, blocks)).astype(jnp.int32))
    lines.append(jnp.zeros((8 - len(lines), blocks), jnp.int32))
    return jnp.concatenate(lines, axis=0)


class Exchange:
    def __init__(self, sizes):
        self.sizes = sizes
        dp = lax.axis_index("dp")
        nz, ny, nx = sizes
        self.me = (dp // (ny * nx), (dp // nx) % ny, dp % nx)
        self.sub = lax.axis_index("sub")
        self.sent = []

    def peer(self, axis, step):
        n = self.sizes[axis]
        place = list(self.me)
        place[axis] = lax.rem(place[axis] + (step % n), n)
        return (place[0] * self.sizes[1] + place[1]) * self.sizes[2] + place[2]

    def place(self, axis, step):
        n = self.sizes[axis]
        return lax.rem(self.me[axis] + (step % n), n)

    def copy(self, source, target, send, receive, peer, sub=None):
        made = pltpu.make_async_remote_copy(
            src_ref=source,
            dst_ref=target,
            send_sem=send,
            recv_sem=receive,
            device_id=(peer, self.sub if sub is None else sub),
            device_id_type=MESH,
        )
        made.start()
        self.sent.append(made)
        return made

    def cut(self, axes, units, half=None):
        index = []
        for axis in range(3):
            if axis in axes:
                index.append(axes[axis])
            elif half is not None and axis == half[0]:
                n = self.sizes[axis]
                index.append(pl.ds(half[1] * (n // 2), n // 2))
            else:
                index.append(slice(None))
        index.append(pl.ds(units[0], units[1]))
        return tuple(index)


def ring_scatter(ex, buffer, wire, landing, send, receive, order, units):
    axis = order[0]
    n = ex.sizes[axis]
    halved = 1 if axis == 0 else 0
    table = hop_table(n)
    links = chains(n)
    copies = {}

    def start(number, hop):
        direction, half, hops = links[number]
        target = ex.place(axis, direction * (hops - hop + 1))
        at = table[number, hop]
        copies[number, hop] = ex.copy(
            wire.at[ex.cut({axis: target}, units, (halved, half))],
            landing.at[at],
            send.at[at],
            receive.at[at],
            ex.peer(axis, direction),
        )

    for number in range(len(links)):
        start(number, 1)
    for hop in range(1, n // 2 + 1):
        for number, (direction, half, hops) in enumerate(links):
            if hop > hops:
                continue
            yield
            copies[number, hop].wait_recv()
            target = ex.place(axis, direction * (hops - hop))
            index = ex.cut({axis: target}, units, (halved, half))
            total = buffer[index] + landing[table[number, hop]].astype(F32)
            if hop < hops:
                wire[index] = total.astype(BF16)
                start(number, hop + 1)
            else:
                buffer[index] = total


def direct_scatter(ex, buffer, wire, landing, send, receive, order, stage, units):
    axis = order[stage]
    n = ex.sizes[axis]
    fixed = {a: ex.me[a] for a in order[:stage]}
    copies = []
    for step in range(1, n):
        index = ex.cut({**fixed, axis: ex.place(axis, step)}, units)
        wire[index] = buffer[index].astype(BF16)
        copies.append(
            ex.copy(wire.at[index], landing.at[step - 1], send.at[step - 1], receive.at[step - 1], ex.peer(axis, step))
        )
    yield
    own = ex.cut({**fixed, axis: ex.me[axis]}, units)
    total = buffer[own]
    for step in range(1, n):
        copies[step - 1].wait_recv()
        total = total + landing[step - 1].astype(F32)
    buffer[own] = total


def direct_gather(ex, buffer, send, receive, order, stage, units):
    axis = order[stage]
    n = ex.sizes[axis]
    index = ex.cut({a: ex.me[a] for a in order[: stage + 1]}, units)
    copies = []
    for step in range(1, n):
        copies.append(
            ex.copy(buffer.at[index], buffer.at[index], send.at[step - 1], receive.at[step - 1], ex.peer(axis, step))
        )
    yield
    for made in copies:
        made.wait_recv()


def ring_gather(ex, buffer, send, receive, order, units):
    axis = order[0]
    n = ex.sizes[axis]
    halved = 1 if axis == 0 else 0
    table = hop_table(n)
    links = chains(n)
    copies = {}

    def start(number, hop):
        direction, half, _ = links[number]
        index = ex.cut({axis: ex.place(axis, -direction * (hop - 1))}, units, (halved, half))
        at = table[number, hop]
        copies[number, hop] = ex.copy(
            buffer.at[index], buffer.at[index], send.at[at], receive.at[at], ex.peer(axis, direction)
        )

    for number in range(len(links)):
        start(number, 1)
    for hop in range(1, n // 2 + 1):
        for number, (_, _, hops) in enumerate(links):
            if hop > hops:
                continue
            yield
            copies[number, hop].wait_recv()
            if hop < hops:
                start(number, hop + 1)


def vector_sum(ex, buffer, landing, send, receive):
    at = 0
    for axis in (2, 1, 0):
        n = ex.sizes[axis]
        copies = []
        stage = 2 - axis
        for step in range(1, n):
            slot = at + step - 1
            copies.append(
                ex.copy(buffer.at[stage], landing.at[slot], send.at[slot], receive.at[slot], ex.peer(axis, step))
            )
        yield
        total = buffer[stage]
        for step in range(1, n):
            copies[step - 1].wait_recv()
            total = total + landing[at + step - 1]
        buffer[stage + 1] = total
        at += n - 1


def chain(*parts):
    for part in parts:
        yield from part()


def interleave(*parts):
    live = list(parts)
    while live:
        for part in list(live):
            try:
                next(part)
            except StopIteration:
                live.remove(part)


def drain(part, steps):
    for _ in range(steps):
        try:
            next(part)
        except StopIteration:
            return


def share_kernel(sizes, *refs):
    refs = list(refs)
    take = lambda count: [refs.pop(0) for _ in range(count)]
    grads, errors, vec_grads, q_start, momentum, master, owner = take(7)
    basis_out, right_out, vec_out, slots_out, table_out = take(5)
    raw_g, raw_e, load_sem, work, wire, mean = take(6)
    high = take(1)[0]
    vec_buf, vec_land, vec_send, vec_recv = take(4)
    left_t = take(1)[0]
    mine, theirs, core_send, core_recv = take(4)
    basis_mine, basis_theirs = take(2)
    slots_mine = take(1)[0]
    lands, sends, recvs = [], [], []
    for _ in ORDERS:
        lands.append(take(3))
        sends.append(take(9))
        recvs.append(take(9))

    nz, ny, nx = sizes
    ex = Exchange(sizes)
    rank = q_start.shape[1]
    cols = q_start.shape[2]
    groups = cols // LANES
    plane = ny * nx * BLOCK
    per_mat = nz // 2
    dp_count = nz * ny * nx

    barrier = pltpu.get_barrier_semaphore()
    peers = [(ex.peer(axis, step), ex.sub) for axis in range(3) for step in range(1, sizes[axis])]
    peers.append((lax.axis_index("dp"), 1 - ex.sub))
    for peer in peers:
        pl.semaphore_signal(barrier, inc=1, device_id=peer, device_id_type=MESH)

    loads = []
    for z in range(nz):
        rows = pl.ds((z % per_mat) * plane, plane)
        pair = []
        for number, (source, target) in enumerate(((grads, raw_g), (errors, raw_e))):
            made = pltpu.make_async_copy(source.at[0, z // per_mat, rows], target.at[z], load_sem.at[z, number])
            made.start()
            pair.append(made)
        loads.append(pair)

    slots = master[...] - (STEP_RATE * MOMENTUM_DECAY) * momentum[...]
    slots = slots.astype(BF16)
    for slot in range(slots.shape[0]):
        for group in range(2):
            slots_mine[2 * slot + group] = slots[slot, :, group * LANES : (group + 1) * LANES]
    vec_buf[0] = vec_grads[0]
    own_slots = pltpu.make_async_copy(slots_mine, slots_out.at[ex.me[0], ex.me[1], ex.me[2]], load_sem.at[0, 2])
    own_slots.start()

    for z in range(nz):
        for made in loads[z]:
            made.wait()
        mixed = raw_g[z].astype(F32) + raw_e[z].astype(F32)
        for group in range(groups):
            tiles = mixed[:, group * LANES : (group + 1) * LANES].reshape(ny, nx, BLOCK, LANES)
            work[z, :, :, group] = tiles
            wire[z, :, :, group] = tiles.astype(BF16)
    own_slots.wait()

    pl.semaphore_wait(barrier, len(peers))

    scale = 1.0 / dp_count
    gathered = [False] * len(ORDERS)

    def scatter(number):
        order, units, _ = ORDERS[number]
        land, send, recv = lands[number], sends[number], recvs[number]
        yield from ring_scatter(ex, work, wire, land[0], send[0], recv[0], order, units)
        yield from direct_scatter(ex, work, wire, land[1], send[1], recv[1], order, 1, units)
        yield from direct_scatter(ex, work, wire, land[2], send[2], recv[2], order, 2, units)
        own = ex.cut({a: ex.me[a] for a in range(3)}, units)
        mean[own] = (work[own] * scale).astype(BF16)
        yield from direct_gather(ex, mean, send[3], recv[3], order, 2, units)
        yield from direct_gather(ex, mean, send[4], recv[4], order, 1, units)
        yield from ring_gather(ex, mean, send[5], recv[5], order, units)
        assert gathered[number]
        next(spreads[number])

    def early(number):
        order, units = SLOT_ORDERS[number], ORDERS[number][2]
        send, recv = sends[number], recvs[number]
        yield from direct_gather(ex, slots_out, send[6], recv[6], order, 2, units)
        yield from direct_gather(ex, slots_out, send[7], recv[7], order, 1, units)
        gathered[number] = True

    def spread(number):
        order, units = SLOT_ORDERS[number], ORDERS[number][2]
        yield from ring_gather(ex, slots_out, sends[number][8], recvs[number][8], order, units)

    spreads = [spread(number) for number in range(3)]
    interleave(
        *[scatter(number) for number in range(3)],
        vector_sum(ex, vec_buf, vec_land, vec_send, vec_recv),
        *[early(number) for number in range(3)],
    )
    table_out[...] = place_blocks(owner[...], lax.axis_index("dp"), ex.sub, momentum.shape[0])
    vec_out[...] = vec_buf[3] * (VECTOR_RATE / dp_count)

    def advance():
        for part in spreads:
            drain(part, 4)

    for z in range(nz):
        for group in range(groups):
            high[z, :, group * LANES : (group + 1) * LANES] = mean[z, :, :, group].reshape(plane, LANES)

    right_t = [q_start[m] for m in range(2)]
    for step_index in range(ROUNDS):
        for m in range(2):
            q_terms = split3(right_t[m])
            q_all = jnp.concatenate(q_terms, axis=0)
            gram = jnp.zeros((3 * rank, 3 * rank), F32)
            product = jnp.zeros((3 * rank, cols), F32)
            for part in range(per_mat):
                z = m * per_mat + part
                top = high[z]
                wide = nt(q_all, top)
                left = wide[:rank] + (wide[rank : 2 * rank] + wide[2 * rank :])
                left_t[m, :, part * plane : (part + 1) * plane] = left
                p_terms = split3(left)
                p_all = jnp.concatenate(p_terms, axis=0)
                gram = gram + nt(p_all, p_all)
                product = product + nn(p_all, top)
            total = product[:rank] + (product[rank : 2 * rank] + product[2 * rank :])
            mine[step_index, m, :, :cols] = total
            gram_rows = gram[:rank] + (gram[rank : 2 * rank] + gram[2 * rank :])
            square = gram_rows[:, :rank] + (gram_rows[:, rank : 2 * rank] + gram_rows[:, 2 * rank :])
            mine[step_index, m, :, cols:] = jnp.concatenate([square] * (LANES // rank), axis=1)
        made = ex.copy(
            mine.at[step_index],
            theirs.at[step_index],
            core_send.at[step_index],
            core_recv.at[step_index],
            lax.axis_index("dp"),
            1 - ex.sub,
        )
        advance()
        made.wait_recv()
        both = [mine[step_index, m] + theirs[step_index, m] for m in range(2)]
        inverses = inverse_factor(*[both[m][:, cols : cols + rank] for m in range(2)])
        right_t = [
            lax.dot_general(
                inverses[m], both[m][:, :cols], (((1,), (0,)), ((), ())), precision=HIGH, preferred_element_type=F32
            )
            for m in range(2)
        ]
        advance()
    for m in range(2):
        right_out[m] = right_t[m]
        basis_mine[m] = lax.dot_general(
            inverses[m], left_t[m], (((1,), (0,)), ((), ())), precision=HIGH, preferred_element_type=F32
        )
    made = ex.copy(
        basis_mine, basis_theirs, core_send.at[ROUNDS], core_recv.at[ROUNDS], lax.axis_index("dp"), 1 - ex.sub
    )
    for part in spreads:
        drain(part, 64)
    basis_out[ex.sub] = basis_mine[...]
    made.wait_recv()
    basis_out[1 - ex.sub] = basis_theirs[...]
    for made in ex.sent:
        made.wait_send()


def share(sizes, grads, errors, vec_grads, q_start, momentum, master, owner):
    nz, ny, nx = sizes
    mats, rows, cols = grads.shape[1:]
    rank = q_start.shape[1]
    plane = ny * nx * BLOCK
    vmem = pl.BlockSpec(memory_space=pltpu.VMEM)
    anywhere = pl.BlockSpec(memory_space=pl.ANY)
    dma = pltpu.SemaphoreType.DMA
    wires = sum(n - 1 for n in sizes)
    scratch = [
        pltpu.VMEM((nz, plane, cols), BF16),
        pltpu.VMEM((nz, plane, cols), BF16),
        dma((nz, 3)),
        pltpu.VMEM((nz, ny, nx, PARTS, BLOCK, LANES), F32),
        pltpu.VMEM((nz, ny, nx, PARTS, BLOCK, LANES), BF16),
        pltpu.VMEM((nz, ny, nx, PARTS, BLOCK, LANES), BF16),
        pltpu.VMEM((nz, plane, cols), BF16),
        pltpu.VMEM((4,) + vec_grads.shape[1:], F32),
        pltpu.VMEM((wires,) + vec_grads.shape[1:], F32),
        dma((wires,)),
        dma((wires,)),
        pltpu.VMEM((mats, rank, rows), F32),
        pltpu.VMEM((ROUNDS, mats, rank, cols + LANES), F32),
        pltpu.VMEM((ROUNDS, mats, rank, cols + LANES), F32),
        dma((ROUNDS + 1,)),
        dma((ROUNDS + 1,)),
        pltpu.VMEM((mats, rank, rows), F32),
        pltpu.VMEM((mats, rank, rows), F32),
        pltpu.VMEM((UNITS, BLOCK, LANES), BF16),
    ]
    for (order, (_, count), _), slot_order in zip(ORDERS, SLOT_ORDERS):
        first, second, third = order
        halved = 1 if first == 0 else 0
        shape = [sizes[a] // 2 if a == halved else sizes[a] for a in range(3) if a != first]
        hops = len(hop_table(sizes[first]))
        tail = (count, BLOCK, LANES)
        scratch.append(pltpu.VMEM((hops, *shape, *tail), BF16))
        scratch.append(pltpu.VMEM((sizes[second] - 1, sizes[third], *tail), BF16))
        scratch.append(pltpu.VMEM((sizes[third] - 1, *tail), BF16))
        counts = [hops, sizes[second] - 1, sizes[third] - 1]
        counts = counts + counts[::-1] + [sizes[slot_order[2]] - 1, sizes[slot_order[1]] - 1, hops]
        for _ in range(2):
            scratch.extend(dma((n,)) for n in counts)
    return pl.pallas_call(
        functools.partial(share_kernel, sizes),
        out_shape=(
            jax.ShapeDtypeStruct((2, mats, rank, rows), F32),
            jax.ShapeDtypeStruct((mats, rank, cols), F32),
            jax.ShapeDtypeStruct(vec_grads.shape[1:], F32),
            jax.ShapeDtypeStruct((nz, ny, nx, UNITS, BLOCK, LANES), BF16),
            jax.ShapeDtypeStruct((8, owner.shape[1]), jnp.int32),
        ),
        in_specs=[anywhere, anywhere, vmem, vmem, vmem, vmem, vmem],
        out_specs=(vmem, vmem, vmem, anywhere, vmem),
        scratch_shapes=scratch,
        compiler_params=pltpu.CompilerParams(
            collective_id=0, has_side_effects=True, vmem_limit_bytes=56 * 1024 * 1024
        ),
        name="share",
    )(grads, errors, vec_grads, q_start, momentum, master, owner)


def finish_kernel(steps, table, grads, errors, basis, right, gathered, momentum, master, vec, gains, *rest):
    errors_out, new_gains, new_momentum, new_master, weights, approx = rest
    step = pl.program_id(0)
    slots = momentum.shape[0]
    sub = table[1 + slots, 0]
    per_mat = steps // 2
    mat = step // per_mat
    part = lax.rem(step, per_mat)
    rows = grads.shape[2]
    half_cols = weights.shape[2]

    def cat(values, first):
        top, middle, low = split3(values)
        return jnp.concatenate([top, top, middle, low] if first else [top, middle, top, top], axis=0)

    def product(left_t, right_t):
        return lax.dot_general(cat(left_t, True), cat(right_t, False), (((0,), (0,)), ((), ())), preferred_element_type=F32)

    local = basis[sub, mat, :, pl.ds(pl.multiple_of(part * rows, rows), rows)]
    mixed = grads[0, 0].astype(F32) + errors[0, 0].astype(F32)
    errors_out[0, 0] = (mixed - product(local, right[mat])).astype(BF16)

    half = part // (per_mat // 2)
    inner = lax.rem(part, per_mat // 2)
    wide = basis[half, mat, :, pl.ds(pl.multiple_of(inner * 2 * rows, 2 * rows), 2 * rows)]
    columns = right[mat, :, pl.ds(pl.multiple_of(sub * half_cols, half_cols), half_cols)]
    per_step = 2 * rows // BLOCK
    approx[pl.ds(step * per_step, per_step)] = product(wide, columns).reshape(per_step, BLOCK, half_cols)

    for number in range(per_step):
        block = step * per_step + number
        at = table[0, block]
        for group in range(half_cols // LANES):
            lanes = slice(group * LANES, (group + 1) * LANES)
            value = gathered[at, group].astype(F32) - STEP_RATE * approx[block, :, lanes]
            weights[0, number * BLOCK : (number + 1) * BLOCK, lanes] = value.astype(BF16)

    @pl.when(step == steps - 1)
    def _():
        new_gains[...] = gains[...] - vec[...]
        for slot in range(slots):
            block = table[1 + slot, 0]
            valid = block >= 0
            moved = MOMENTUM_DECAY * momentum[slot] + approx[jnp.maximum(block, 0)]
            moved = jnp.where(valid, moved, 0.0)
            new_momentum[slot] = moved
            new_master[slot] = jnp.where(valid, master[slot] - STEP_RATE * moved, 0.0)


def finish(steps, table, grads, errors, basis, right, gathered, momentum, master, vec, gains):
    mats, rows, cols = grads.shape[1:]
    blocks = 2 * mats * rows // BLOCK
    half_cols = momentum.shape[2]
    per_mat = steps // 2
    chunk = rows // per_mat
    moving = lambda i, t: (0, i // per_mat, i % per_mat, 0)
    whole = lambda shape: pl.BlockSpec(shape, lambda i, t: (0,) * len(shape))
    return pl.pallas_call(
        functools.partial(finish_kernel, steps),
        grid_spec=pltpu.PrefetchScalarGridSpec(
            num_scalar_prefetch=1,
            grid=(steps,),
            in_specs=[
                pl.BlockSpec((1, 1, chunk, cols), moving),
                pl.BlockSpec((1, 1, chunk, cols), moving),
                whole(basis.shape),
                whole(right.shape),
                whole(gathered.shape),
                whole(momentum.shape),
                whole(master.shape),
                whole(vec.shape),
                whole(gains.shape),
            ],
            out_specs=[
                pl.BlockSpec((1, 1, chunk, cols), moving),
                whole(gains.shape),
                whole(momentum.shape),
                whole(master.shape),
                pl.BlockSpec((1, 2 * chunk, half_cols), lambda i, t: (i // per_mat, i % per_mat, 0)),
            ],
            scratch_shapes=[pltpu.VMEM((blocks, BLOCK, half_cols), F32)],
        ),
        out_shape=(
            jax.ShapeDtypeStruct(grads.shape, BF16),
            jax.ShapeDtypeStruct(gains.shape, F32),
            jax.ShapeDtypeStruct(momentum.shape, F32),
            jax.ShapeDtypeStruct(master.shape, F32),
            jax.ShapeDtypeStruct((mats, 2 * rows, half_cols), BF16),
        ),
        compiler_params=pltpu.CompilerParams(vmem_limit_bytes=56 * 1024 * 1024),
        name="finish",
    )(table, grads, errors, basis, right, gathered, momentum, master, vec, gains)


def body(grads, errors, vec_grads, gains, q_start, owner, momentum, master):
    replicas = lax.axis_size("dp")
    sizes = torus(replicas)
    slots = momentum.shape[0]
    basis, right, vec, gathered, table = share(
        sizes, grads, errors, vec_grads, jnp.swapaxes(q_start, 1, 2), momentum, master, owner[None]
    )
    gathered = gathered.reshape(replicas * slots, 2, BLOCK, LANES)
    errors_out, new_gains, new_momentum, new_master, weights = finish(
        sizes[0], table, grads, errors, basis, right, gathered, momentum, master, vec, gains
    )
    return (errors_out, new_gains, new_momentum, new_master, weights)


def solution(mesh):
    placed = (
        P("dp", None, "sub", None),
        P("dp", None, "sub", None),
        P("dp", None, "sub"),
        P(None, "sub"),
        P(),
        P(),
        P("dp", None, "sub"),
        P("dp", None, "sub"),
    )
    return jax.shard_map(
        body,
        mesh=mesh,
        in_specs=placed,
        out_specs=(
            P("dp", None, "sub", None),
            P(None, "sub"),
            P("dp", None, "sub"),
            P("dp", None, "sub"),
            P(None, None, "sub"),
        ),
        check_vma=False,
    )
```

```python
import functools

import jax
import jax.numpy as jnp
from jax import lax
from jax.experimental import pallas as pl
from jax.experimental.pallas import tpu as pltpu
from jax.sharding import PartitionSpec as P

MESH = pl.DeviceIdType.MESH
F32 = jnp.float32
BF16 = jnp.bfloat16
HIGH = lax.Precision.HIGHEST

ROUNDS = 2
MOMENTUM_DECAY = 0.9
STEP_RATE = 0.5
VECTOR_RATE = 1.0

LANES = 128
BLOCK = 16
UNITS = 8
STRIDE = 8
PARTS = 4

SLOT_ORDERS = ((2, 1, 0), (1, 2, 0), (0, 2, 1))

ORDERS = (((2, 1, 0), (0, 2), (0, 3)), ((1, 0, 2), (2, 1), (3, 3)), ((0, 2, 1), (3, 1), (6, 2)))


def torus(dp):
    return {128: (8, 4, 4), 16: (4, 2, 2), 8: (2, 2, 2)}[dp]


def split3(value):
    high = value.astype(BF16)
    rest = value - high.astype(F32)
    middle = rest.astype(BF16)
    low = (rest - middle.astype(F32)).astype(BF16)
    return high, middle, low


def nt(a, b):
    return lax.dot_general(a, b, (((1,), (1,)), ((), ())), preferred_element_type=F32)


def nn(a, b):
    return lax.dot_general(a, b, (((1,), (0,)), ((), ())), preferred_element_type=F32)


def chains(n):
    found = []
    for longer in (True, False):
        for direction in (1, -1):
            half = 0 if (direction == 1) == longer else 1
            hops = n // 2 if longer else n // 2 - 1
            if hops:
                found.append((direction, half, hops))
    return found


def hop_table(n):
    table = {}
    for number, (_, _, hops) in enumerate(chains(n)):
        for hop in range(1, hops + 1):
            table[number, hop] = len(table)
    return table


def inverse_factor(gram0, gram1):
    rank = gram0.shape[0]
    rows = lax.broadcasted_iota(jnp.int32, (rank, LANES), 0)
    lanes = lax.broadcasted_iota(jnp.int32, (rank, LANES), 1)
    eye = (lax.broadcasted_iota(jnp.int32, (rank, rank), 0) == lax.broadcasted_iota(jnp.int32, (rank, rank), 1)).astype(F32)
    table = jnp.concatenate([gram0, eye, gram1, eye], axis=1)
    first = lanes < 2 * rank
    pivots = jnp.ones((rank, LANES), F32)
    for k in range(0, rank, STRIDE):
        columns, lines = [], []
        for j in range(k, k + STRIDE):
            columns.append(jnp.where(first, table[:, j : j + 1], table[:, 2 * rank + j : 2 * rank + j + 1]))
            lines.append(table[j : j + 1, :])
        change = jnp.zeros((rank, LANES), F32)
        for j in range(STRIDE):
            pivot = columns[j][k + j : k + j + 1, :]
            pivots = jnp.where(rows == k + j, pivot, pivots)
            inverse = 1.0 / pivot
            scaled = lines[j] * inverse
            for i in range(j + 1, STRIDE):
                factor = columns[j][k + i : k + i + 1, :]
                lines[i] = lines[i] - factor * scaled
                columns[i] = columns[i] - columns[j] * (factor * inverse)
            change = change + jnp.where(rows > k + j, columns[j] * scaled, 0.0)
        table = table - change
    table = table * lax.rsqrt(pivots)
    return table[:, rank : 2 * rank], table[:, 3 * rank : 4 * rank]


def place_blocks(owner, dp, sub, slots):
    blocks = owner.shape[1]
    wide = jnp.broadcast_to(owner.astype(F32), (blocks, blocks))
    before = lax.broadcasted_iota(jnp.int32, wide.shape, 0)
    block = lax.broadcasted_iota(jnp.int32, wide.shape, 1)
    rank = jnp.sum(jnp.where((wide == wide.T) & (before < block), 1.0, 0.0), axis=0, keepdims=True)
    rank = rank.astype(jnp.int32)
    lines = [owner * slots + rank]
    for slot in range(slots):
        held = jnp.where((owner == dp) & (rank == slot), block[:1] + 1, 0).astype(F32)
        held = jnp.sum(held, axis=1, keepdims=True).astype(jnp.int32) - 1
        lines.append(jnp.broadcast_to(held, (1, blocks)))
    lines.append(jnp.broadcast_to(sub, (1, blocks)).astype(jnp.int32))
    lines.append(jnp.zeros((8 - len(lines), blocks), jnp.int32))
    return jnp.concatenate(lines, axis=0)


class Exchange:
    def __init__(self, sizes):
        self.sizes = sizes
        dp = lax.axis_index("dp")
        nz, ny, nx = sizes
        self.me = (dp // (ny * nx), (dp // nx) % ny, dp % nx)
        self.sub = lax.axis_index("sub")
        self.sent = []

    def peer(self, axis, step):
        n = self.sizes[axis]
        place = list(self.me)
        place[axis] = lax.rem(place[axis] + (step % n), n)
        return (place[0] * self.sizes[1] + place[1]) * self.sizes[2] + place[2]

    def place(self, axis, step):
        n = self.sizes[axis]
        return lax.rem(self.me[axis] + (step % n), n)

    def copy(self, source, target, send, receive, peer, sub=None):
        made = pltpu.make_async_remote_copy(
            src_ref=source,
            dst_ref=target,
            send_sem=send,
            recv_sem=receive,
            device_id=(peer, self.sub if sub is None else sub),
            device_id_type=MESH,
        )
        made.start()
        self.sent.append(made)
        return made

    def cut(self, axes, units, half=None):
        index = []
        for axis in range(3):
            if axis in axes:
                index.append(axes[axis])
            elif half is not None and axis == half[0]:
                n = self.sizes[axis]
                index.append(pl.ds(half[1] * (n // 2), n // 2))
            else:
                index.append(slice(None))
        index.append(pl.ds(units[0], units[1]))
        return tuple(index)


def ring_scatter(ex, buffer, wire, landing, send, receive, order, units):
    axis = order[0]
    n = ex.sizes[axis]
    halved = 1 if axis == 0 else 0
    table = hop_table(n)
    links = chains(n)
    copies = {}

    def start(number, hop):
        direction, half, hops = links[number]
        target = ex.place(axis, direction * (hops - hop + 1))
        at = table[number, hop]
        copies[number, hop] = ex.copy(
            wire.at[ex.cut({axis: target}, units, (halved, half))],
            landing.at[at],
            send.at[at],
            receive.at[at],
            ex.peer(axis, direction),
        )

    for number in range(len(links)):
        start(number, 1)
    for hop in range(1, n // 2 + 1):
        for number, (direction, half, hops) in enumerate(links):
            if hop > hops:
                continue
            yield
            copies[number, hop].wait_recv()
            target = ex.place(axis, direction * (hops - hop))
            index = ex.cut({axis: target}, units, (halved, half))
            total = buffer[index] + landing[table[number, hop]].astype(F32)
            if hop < hops:
                wire[index] = total.astype(BF16)
                start(number, hop + 1)
            else:
                buffer[index] = total


def direct_scatter(ex, buffer, wire, landing, send, receive, order, stage, units):
    axis = order[stage]
    n = ex.sizes[axis]
    fixed = {a: ex.me[a] for a in order[:stage]}
    copies = []
    for step in range(1, n):
        index = ex.cut({**fixed, axis: ex.place(axis, step)}, units)
        wire[index] = buffer[index].astype(BF16)
        copies.append(
            ex.copy(wire.at[index], landing.at[step - 1], send.at[step - 1], receive.at[step - 1], ex.peer(axis, step))
        )
    yield
    own = ex.cut({**fixed, axis: ex.me[axis]}, units)
    total = buffer[own]
    for step in range(1, n):
        copies[step - 1].wait_recv()
        total = total + landing[step - 1].astype(F32)
    buffer[own] = total


def direct_gather(ex, buffer, send, receive, order, stage, units):
    axis = order[stage]
    n = ex.sizes[axis]
    index = ex.cut({a: ex.me[a] for a in order[: stage + 1]}, units)
    copies = []
    for step in range(1, n):
        copies.append(
            ex.copy(buffer.at[index], buffer.at[index], send.at[step - 1], receive.at[step - 1], ex.peer(axis, step))
        )
    yield
    for made in copies:
        made.wait_recv()


def ring_gather(ex, buffer, send, receive, order, units):
    axis = order[0]
    n = ex.sizes[axis]
    halved = 1 if axis == 0 else 0
    table = hop_table(n)
    links = chains(n)
    copies = {}

    def start(number, hop):
        direction, half, _ = links[number]
        index = ex.cut({axis: ex.place(axis, -direction * (hop - 1))}, units, (halved, half))
        at = table[number, hop]
        copies[number, hop] = ex.copy(
            buffer.at[index], buffer.at[index], send.at[at], receive.at[at], ex.peer(axis, direction)
        )

    for number in range(len(links)):
        start(number, 1)
    for hop in range(1, n // 2 + 1):
        for number, (_, _, hops) in enumerate(links):
            if hop > hops:
                continue
            yield
            copies[number, hop].wait_recv()
            if hop < hops:
                start(number, hop + 1)


def vector_sum(ex, buffer, landing, send, receive):
    at = 0
    for axis in (2, 1, 0):
        n = ex.sizes[axis]
        copies = []
        stage = 2 - axis
        for step in range(1, n):
            slot = at + step - 1
            copies.append(
                ex.copy(buffer.at[stage], landing.at[slot], send.at[slot], receive.at[slot], ex.peer(axis, step))
            )
        yield
        total = buffer[stage]
        for step in range(1, n):
            copies[step - 1].wait_recv()
            total = total + landing[at + step - 1]
        buffer[stage + 1] = total
        at += n - 1


def chain(*parts):
    for part in parts:
        yield from part()


def interleave(*parts):
    live = list(parts)
    while live:
        for part in list(live):
            try:
                next(part)
            except StopIteration:
                live.remove(part)


def drain(part, steps):
    for _ in range(steps):
        try:
            next(part)
        except StopIteration:
            return


def share_kernel(sizes, *refs):
    refs = list(refs)
    take = lambda count: [refs.pop(0) for _ in range(count)]
    grads, errors, vec_grads, q_start, momentum, master, owner = take(7)
    basis_out, right_out, vec_out, slots_out, table_out = take(5)
    raw_g, raw_e, load_sem, work, wire, mean = take(6)
    high = take(1)[0]
    vec_buf, vec_land, vec_send, vec_recv = take(4)
    left_t = take(1)[0]
    mine, theirs, core_send, core_recv = take(4)
    basis_mine, basis_theirs = take(2)
    slots_mine = take(1)[0]
    lands, sends, recvs = [], [], []
    for _ in ORDERS:
        lands.append(take(3))
        sends.append(take(9))
        recvs.append(take(9))

    nz, ny, nx = sizes
    ex = Exchange(sizes)
    rank = q_start.shape[1]
    cols = q_start.shape[2]
    groups = cols // LANES
    plane = ny * nx * BLOCK
    per_mat = nz // 2
    dp_count = nz * ny * nx

    barrier = pltpu.get_barrier_semaphore()
    peers = [(ex.peer(axis, step), ex.sub) for axis in range(3) for step in range(1, sizes[axis])]
    peers.append((lax.axis_index("dp"), 1 - ex.sub))
    for peer in peers:
        pl.semaphore_signal(barrier, inc=1, device_id=peer, device_id_type=MESH)

    loads = []
    for z in range(nz):
        rows = pl.ds((z % per_mat) * plane, plane)
        pair = []
        for number, (source, target) in enumerate(((grads, raw_g), (errors, raw_e))):
            made = pltpu.make_async_copy(source.at[0, z // per_mat, rows], target.at[z], load_sem.at[z, number])
            made.start()
            pair.append(made)
        loads.append(pair)

    slots = master[...] - (STEP_RATE * MOMENTUM_DECAY) * momentum[...]
    slots = slots.astype(BF16)
    for slot in range(slots.shape[0]):
        for group in range(2):
            slots_mine[2 * slot + group] = slots[slot, :, group * LANES : (group + 1) * LANES]
    vec_buf[0] = vec_grads[0]
    own_slots = pltpu.make_async_copy(slots_mine, slots_out.at[ex.me[0], ex.me[1], ex.me[2]], load_sem.at[0, 2])
    own_slots.start()

    for z in range(nz):
        for made in loads[z]:
            made.wait()
        mixed = raw_g[z].astype(F32) + raw_e[z].astype(F32)
        for group in range(groups):
            tiles = mixed[:, group * LANES : (group + 1) * LANES].reshape(ny, nx, BLOCK, LANES)
            work[z, :, :, group] = tiles
            wire[z, :, :, group] = tiles.astype(BF16)
    own_slots.wait()

    pl.semaphore_wait(barrier, len(peers))

    scale = 1.0 / dp_count
    gathered = [False] * len(ORDERS)

    def scatter(number):
        order, units, _ = ORDERS[number]
        land, send, recv = lands[number], sends[number], recvs[number]
        yield from ring_scatter(ex, work, wire, land[0], send[0], recv[0], order, units)
        yield from direct_scatter(ex, work, wire, land[1], send[1], recv[1], order, 1, units)
        yield from direct_scatter(ex, work, wire, land[2], send[2], recv[2], order, 2, units)
        own = ex.cut({a: ex.me[a] for a in range(3)}, units)
        mean[own] = (work[own] * scale).astype(BF16)
        yield from direct_gather(ex, mean, send[3], recv[3], order, 2, units)
        yield from direct_gather(ex, mean, send[4], recv[4], order, 1, units)
        yield from ring_gather(ex, mean, send[5], recv[5], order, units)
        assert gathered[number]
        next(spreads[number])

    def early(number):
        order, units = SLOT_ORDERS[number], ORDERS[number][2]
        send, recv = sends[number], recvs[number]
        yield from direct_gather(ex, slots_out, send[6], recv[6], order, 2, units)
        yield from direct_gather(ex, slots_out, send[7], recv[7], order, 1, units)
        gathered[number] = True

    def spread(number):
        order, units = SLOT_ORDERS[number], ORDERS[number][2]
        yield from ring_gather(ex, slots_out, sends[number][8], recvs[number][8], order, units)

    def tabulate():
        yield
        table_out[...] = place_blocks(owner[...], lax.axis_index("dp"), ex.sub, momentum.shape[0])

    spreads = [spread(number) for number in range(3)]
    interleave(
        *[scatter(number) for number in range(3)],
        vector_sum(ex, vec_buf, vec_land, vec_send, vec_recv),
        *[early(number) for number in range(3)],
        tabulate(),
    )
    vec_out[...] = vec_buf[3] * (VECTOR_RATE / dp_count)

    def advance():
        for part in spreads:
            drain(part, 4)

    for z in range(nz):
        for group in range(groups):
            high[z, :, group * LANES : (group + 1) * LANES] = mean[z, :, :, group].reshape(plane, LANES)

    right_t = [q_start[m] for m in range(2)]
    for step_index in range(ROUNDS):
        for m in range(2):
            q_terms = split3(right_t[m])
            q_all = jnp.concatenate(q_terms, axis=0)
            gram = jnp.zeros((3 * rank, 3 * rank), F32)
            product = jnp.zeros((3 * rank, cols), F32)
            for part in range(per_mat):
                z = m * per_mat + part
                top = high[z]
                wide = nt(q_all, top)
                left = wide[:rank] + (wide[rank : 2 * rank] + wide[2 * rank :])
                left_t[m, :, part * plane : (part + 1) * plane] = left
                p_terms = split3(left)
                p_all = jnp.concatenate(p_terms, axis=0)
                gram = gram + nt(p_all, p_all)
                product = product + nn(p_all, top)
            total = product[:rank] + (product[rank : 2 * rank] + product[2 * rank :])
            mine[step_index, m, :, :cols] = total
            gram_rows = gram[:rank] + (gram[rank : 2 * rank] + gram[2 * rank :])
            square = gram_rows[:, :rank] + (gram_rows[:, rank : 2 * rank] + gram_rows[:, 2 * rank :])
            mine[step_index, m, :, cols:] = jnp.concatenate([square] * (LANES // rank), axis=1)
        made = ex.copy(
            mine.at[step_index],
            theirs.at[step_index],
            core_send.at[step_index],
            core_recv.at[step_index],
            lax.axis_index("dp"),
            1 - ex.sub,
        )
        advance()
        made.wait_recv()
        both = [mine[step_index, m] + theirs[step_index, m] for m in range(2)]
        inverses = inverse_factor(*[both[m][:, cols : cols + rank] for m in range(2)])
        right_t = [
            lax.dot_general(
                inverses[m], both[m][:, :cols], (((1,), (0,)), ((), ())), precision=HIGH, preferred_element_type=F32
            )
            for m in range(2)
        ]
        advance()
    for m in range(2):
        right_out[m] = right_t[m]
        basis_mine[m] = lax.dot_general(
            inverses[m], left_t[m], (((1,), (0,)), ((), ())), precision=HIGH, preferred_element_type=F32
        )
    made = ex.copy(
        basis_mine, basis_theirs, core_send.at[ROUNDS], core_recv.at[ROUNDS], lax.axis_index("dp"), 1 - ex.sub
    )
    for part in spreads:
        drain(part, 64)
    basis_out[ex.sub] = basis_mine[...]
    made.wait_recv()
    basis_out[1 - ex.sub] = basis_theirs[...]
    for made in ex.sent:
        made.wait_send()


def share(sizes, grads, errors, vec_grads, q_start, momentum, master, owner):
    nz, ny, nx = sizes
    mats, rows, cols = grads.shape[1:]
    rank = q_start.shape[1]
    plane = ny * nx * BLOCK
    vmem = pl.BlockSpec(memory_space=pltpu.VMEM)
    anywhere = pl.BlockSpec(memory_space=pl.ANY)
    dma = pltpu.SemaphoreType.DMA
    wires = sum(n - 1 for n in sizes)
    scratch = [
        pltpu.VMEM((nz, plane, cols), BF16),
        pltpu.VMEM((nz, plane, cols), BF16),
        dma((nz, 3)),
        pltpu.VMEM((nz, ny, nx, PARTS, BLOCK, LANES), F32),
        pltpu.VMEM((nz, ny, nx, PARTS, BLOCK, LANES), BF16),
        pltpu.VMEM((nz, ny, nx, PARTS, BLOCK, LANES), BF16),
        pltpu.VMEM((nz, plane, cols), BF16),
        pltpu.VMEM((4,) + vec_grads.shape[1:], F32),
        pltpu.VMEM((wires,) + vec_grads.shape[1:], F32),
        dma((wires,)),
        dma((wires,)),
        pltpu.VMEM((mats, rank, rows), F32),
        pltpu.VMEM((ROUNDS, mats, rank, cols + LANES), F32),
        pltpu.VMEM((ROUNDS, mats, rank, cols + LANES), F32),
        dma((ROUNDS + 1,)),
        dma((ROUNDS + 1,)),
        pltpu.VMEM((mats, rank, rows), F32),
        pltpu.VMEM((mats, rank, rows), F32),
        pltpu.VMEM((UNITS, BLOCK, LANES), BF16),
    ]
    for (order, (_, count), _), slot_order in zip(ORDERS, SLOT_ORDERS):
        first, second, third = order
        halved = 1 if first == 0 else 0
        shape = [sizes[a] // 2 if a == halved else sizes[a] for a in range(3) if a != first]
        hops = len(hop_table(sizes[first]))
        tail = (count, BLOCK, LANES)
        scratch.append(pltpu.VMEM((hops, *shape, *tail), BF16))
        scratch.append(pltpu.VMEM((sizes[second] - 1, sizes[third], *tail), BF16))
        scratch.append(pltpu.VMEM((sizes[third] - 1, *tail), BF16))
        counts = [hops, sizes[second] - 1, sizes[third] - 1]
        counts = counts + counts[::-1] + [sizes[slot_order[2]] - 1, sizes[slot_order[1]] - 1, hops]
        for _ in range(2):
            scratch.extend(dma((n,)) for n in counts)
    return pl.pallas_call(
        functools.partial(share_kernel, sizes),
        out_shape=(
            jax.ShapeDtypeStruct((2, mats, rank, rows), F32),
            jax.ShapeDtypeStruct((mats, rank, cols), F32),
            jax.ShapeDtypeStruct(vec_grads.shape[1:], F32),
            jax.ShapeDtypeStruct((nz, ny, nx, UNITS, BLOCK, LANES), BF16),
            jax.ShapeDtypeStruct((8, owner.shape[1]), jnp.int32),
        ),
        in_specs=[anywhere, anywhere, vmem, vmem, vmem, vmem, vmem],
        out_specs=(vmem, vmem, vmem, anywhere, vmem),
        scratch_shapes=scratch,
        compiler_params=pltpu.CompilerParams(
            collective_id=0, has_side_effects=True, vmem_limit_bytes=56 * 1024 * 1024
        ),
        name="share",
    )(grads, errors, vec_grads, q_start, momentum, master, owner)


def finish_kernel(steps, table, grads, errors, basis, right, gathered, momentum, master, vec, gains, *rest):
    errors_out, new_gains, new_momentum, new_master, weights, approx = rest
    step = pl.program_id(0)
    slots = momentum.shape[0]
    sub = table[1 + slots, 0]
    per_mat = steps // 2
    mat = step // per_mat
    part = lax.rem(step, per_mat)
    rows = grads.shape[2]
    half_cols = weights.shape[2]

    def cat(values, first):
        top, middle, low = split3(values)
        return jnp.concatenate([top, top, middle, low] if first else [top, middle, top, top], axis=0)

    def product(left_t, right_t):
        return lax.dot_general(cat(left_t, True), cat(right_t, False), (((0,), (0,)), ((), ())), preferred_element_type=F32)

    local = basis[sub, mat, :, pl.ds(pl.multiple_of(part * rows, rows), rows)]
    mixed = grads[0, 0].astype(F32) + errors[0, 0].astype(F32)
    errors_out[0, 0] = (mixed - product(local, right[mat])).astype(BF16)

    half = part // (per_mat // 2)
    inner = lax.rem(part, per_mat // 2)
    wide = basis[half, mat, :, pl.ds(pl.multiple_of(inner * 2 * rows, 2 * rows), 2 * rows)]
    columns = right[mat, :, pl.ds(pl.multiple_of(sub * half_cols, half_cols), half_cols)]
    per_step = 2 * rows // BLOCK
    approx[pl.ds(step * per_step, per_step)] = product(wide, columns).reshape(per_step, BLOCK, half_cols)

    for number in range(per_step):
        block = step * per_step + number
        at = table[0, block]
        for group in range(half_cols // LANES):
            lanes = slice(group * LANES, (group + 1) * LANES)
            value = gathered[at, group].astype(F32) - STEP_RATE * approx[block, :, lanes]
            weights[0, number * BLOCK : (number + 1) * BLOCK, lanes] = value.astype(BF16)

    @pl.when(step == steps - 1)
    def _():
        new_gains[...] = gains[...] - vec[...]
        for slot in range(slots):
            block = table[1 + slot, 0]
            valid = block >= 0
            moved = MOMENTUM_DECAY * momentum[slot] + approx[jnp.maximum(block, 0)]
            moved = jnp.where(valid, moved, 0.0)
            new_momentum[slot] = moved
            new_master[slot] = jnp.where(valid, master[slot] - STEP_RATE * moved, 0.0)


def finish(steps, table, grads, errors, basis, right, gathered, momentum, master, vec, gains):
    mats, rows, cols = grads.shape[1:]
    blocks = 2 * mats * rows // BLOCK
    half_cols = momentum.shape[2]
    per_mat = steps // 2
    chunk = rows // per_mat
    moving = lambda i, t: (0, i // per_mat, i % per_mat, 0)
    whole = lambda shape: pl.BlockSpec(shape, lambda i, t: (0,) * len(shape))
    return pl.pallas_call(
        functools.partial(finish_kernel, steps),
        grid_spec=pltpu.PrefetchScalarGridSpec(
            num_scalar_prefetch=1,
            grid=(steps,),
            in_specs=[
                pl.BlockSpec((1, 1, chunk, cols), moving),
                pl.BlockSpec((1, 1, chunk, cols), moving),
                whole(basis.shape),
                whole(right.shape),
                whole(gathered.shape),
                whole(momentum.shape),
                whole(master.shape),
                whole(vec.shape),
                whole(gains.shape),
            ],
            out_specs=[
                pl.BlockSpec((1, 1, chunk, cols), moving),
                whole(gains.shape),
                whole(momentum.shape),
                whole(master.shape),
                pl.BlockSpec((1, 2 * chunk, half_cols), lambda i, t: (i // per_mat, i % per_mat, 0)),
            ],
            scratch_shapes=[pltpu.VMEM((blocks, BLOCK, half_cols), F32)],
        ),
        out_shape=(
            jax.ShapeDtypeStruct(grads.shape, BF16),
            jax.ShapeDtypeStruct(gains.shape, F32),
            jax.ShapeDtypeStruct(momentum.shape, F32),
            jax.ShapeDtypeStruct(master.shape, F32),
            jax.ShapeDtypeStruct((mats, 2 * rows, half_cols), BF16),
        ),
        compiler_params=pltpu.CompilerParams(vmem_limit_bytes=56 * 1024 * 1024),
        name="finish",
    )(table, grads, errors, basis, right, gathered, momentum, master, vec, gains)


def body(grads, errors, vec_grads, gains, q_start, owner, momentum, master):
    replicas = lax.axis_size("dp")
    sizes = torus(replicas)
    slots = momentum.shape[0]
    basis, right, vec, gathered, table = share(
        sizes, grads, errors, vec_grads, jnp.swapaxes(q_start, 1, 2), momentum, master, owner[None]
    )
    gathered = gathered.reshape(replicas * slots, 2, BLOCK, LANES)
    errors_out, new_gains, new_momentum, new_master, weights = finish(
        sizes[0], table, grads, errors, basis, right, gathered, momentum, master, vec, gains
    )
    return (errors_out, new_gains, new_momentum, new_master, weights)


def solution(mesh):
    placed = (
        P("dp", None, "sub", None),
        P("dp", None, "sub", None),
        P("dp", None, "sub"),
        P(None, "sub"),
        P(),
        P(),
        P("dp", None, "sub"),
        P("dp", None, "sub"),
    )
    return jax.shard_map(
        body,
        mesh=mesh,
        in_specs=placed,
        out_specs=(
            P("dp", None, "sub", None),
            P(None, "sub"),
            P("dp", None, "sub"),
            P("dp", None, "sub"),
            P(None, None, "sub"),
        ),
        check_vma=False,
    )
```
